512 devices in a mesh: pipe: 32 (over y, z_lo, core), dp: 16 (over x, z_hi).
Axes of the slice: x: 4, y: 4, z: 16 (z_hi: 4, z_lo: 4; z = z_hi * 4 + z_lo), core: 2. Of those that a mesh axis runs over, the one named last changes fastest.
Arguments:
- section_inputs: bfloat16 [32, 2, 1024, 4096], P('pipe', None, 'dp'), may hold values from -6 to 6
- arriving: bfloat16 [32, 1024, 4096], P('pipe', 'dp'), may hold values from -2.5 to 2.5
- top_grads: bfloat16 [1, 1024, 4096], P(None, 'dp', 'pipe'), may hold values from -2.5 to 2.5
- project_weights: bfloat16 [32, 4096, 384], P('pipe', 'dp'), may hold values from -0.09375 to 0.09375
- output_weights: bfloat16 [32, 4096, 128], P('pipe', 'dp'), may hold values from -0.5 to 0.5
Outputs:
- project_grads: float32 [32, 4096, 384], P('pipe', 'dp')
- output_grads: float32 [32, 4096, 128], P('pipe', 'dp')
- passed_back: bfloat16 [32, 1024, 4096], P('pipe', 'dp')
The draws below stay inside these ranges and needn't reach their ends.
All inputs are finite; a program needn't handle non-finite values.
Results may differ from the reference program's by a relative error of at most 0.015.
Values may be sent and summed in bfloat16 or wider, within the bound.
A program may use at most 64 MiB of HBM per device.

```python
import math
import jax
import jax.numpy as jnp
from jax import lax

D = 4096
HD = 128
SEQ = 64
TICKS = 2
ROWS = 1024
N_PIPE = 32
N_DP = 16


def levels(stream_key, shape, split, low, largest):
    def one(dim, parts):
        draws = jax.random.uniform(jax.random.fold_in(jax.random.fold_in(stream_key, 6), dim), (parts,), jnp.float32, low / len(split), largest / len(split))
        return jnp.repeat(jnp.exp(draws), shape[dim] // parts).reshape((-1,) + (1,) * (len(shape) - dim - 1))

    factor_of = one(*split[0])
    for cut in split[1:]:
        factor_of = factor_of * one(*cut)
    return factor_of


def noise(key, dims, scale, reach, shards=(), kind=jnp.bfloat16):
    result = jax.random.normal(key, dims, jnp.float32) * scale
    if len(shards) > 0:
        result = levels(key, dims, shards, -0.22, 0.18) * result
    return jnp.clip(result, min=-reach, max=reach).astype(kind)


def setup_inputs(seed: int = 0) -> dict:
    streams_of = jax.random.split(jax.random.key(seed), 6)
    section_inputs = noise(streams_of[0], (N_PIPE, TICKS, ROWS, D), 1.0, 6.0, ((0, 32), (2, 16)))
    arriving = noise(streams_of[1], (N_PIPE, ROWS, D), 0.25, 2.5, ((0, 32), (1, 16)))
    top_grads = noise(streams_of[2], (TICKS - 1, ROWS, D), 0.25, 2.5, ((1, 16), (2, 32)))
    project_weights = noise(streams_of[3], (N_PIPE, D, 3 * HD), D ** -0.5, 0.09375, ((0, 32), (1, 16)))
    output_weights = noise(streams_of[4], (N_PIPE, D, HD), HD ** -0.5, 0.5, ((0, 32), (1, 16)))
    return dict(section_inputs=section_inputs, arriving=arriving, top_grads=top_grads, project_weights=project_weights, output_weights=output_weights)


EPSILON = 1e-06

def normalize(values):
    centered = values - lax.optimization_barrier(jnp.mean(values, axis=-1, keepdims=True))
    inverse = lax.rsqrt(lax.optimization_barrier(jnp.mean(centered * centered, axis=-1, keepdims=True)) + EPSILON)
    return (centered * inverse, inverse)

def norm_back(gradient, normed, inverse):
    centered = gradient - lax.optimization_barrier(jnp.mean(gradient, axis=-1, keepdims=True))
    return inverse * (centered - normed * lax.optimization_barrier(jnp.mean(gradient * normed, axis=-1, keepdims=True)))

def section_tick(inputs, incoming, project_weights, output_weights):
    head_size = output_weights.shape[1]
    root_size = math.sqrt(head_size)
    normed, inverse = normalize(inputs.astype(jnp.float32))
    hidden = normed.astype(jnp.bfloat16)
    projected = jnp.dot(hidden, project_weights, preferred_element_type=jnp.float32)
    query, query_scale = normalize(projected[:, :head_size])
    key_normed, key_scale = normalize(projected[:, head_size:2 * head_size])
    query_half = query.astype(jnp.bfloat16)
    key_half = key_normed.astype(jnp.bfloat16)
    value_half = projected[:, 2 * head_size:].astype(jnp.bfloat16)
    scores = jnp.dot(query_half, key_half.T, preferred_element_type=jnp.float32) / root_size
    powered = jnp.exp(scores)
    attention = powered / lax.optimization_barrier(jnp.sum(powered, axis=-1, keepdims=True))
    attention_half = attention.astype(jnp.bfloat16)
    mixed_half = jnp.dot(attention_half, value_half, preferred_element_type=jnp.float32).astype(jnp.bfloat16)
    head_grad = jnp.dot(incoming, output_weights, preferred_element_type=jnp.float32).astype(jnp.bfloat16)
    prob_grad = jnp.dot(head_grad, value_half.T, preferred_element_type=jnp.float32)
    value_grad = jnp.dot(attention_half.T, head_grad, preferred_element_type=jnp.float32).astype(jnp.bfloat16)
    score_grad = (attention * (prob_grad - lax.optimization_barrier(jnp.sum(attention * prob_grad, axis=-1, keepdims=True))) / root_size).astype(jnp.bfloat16)
    query_grad = jnp.dot(score_grad, key_half, preferred_element_type=jnp.float32)
    key_grad = jnp.dot(score_grad.T, query_half, preferred_element_type=jnp.float32)
    normed_grads = jnp.concatenate([norm_back(query_grad, query, query_scale), norm_back(key_grad, key_normed, key_scale)], axis=1).astype(jnp.bfloat16)
    proj_grad = jnp.concatenate([normed_grads, value_grad], axis=1)
    hidden_grad = jnp.dot(proj_grad, project_weights.T, preferred_element_type=jnp.float32)
    passed = (incoming.astype(jnp.float32) + norm_back(hidden_grad, normed, inverse)).astype(jnp.bfloat16)
    part_project = jnp.dot(hidden.T, proj_grad, preferred_element_type=jnp.float32)
    part_output = jnp.dot(incoming.T, mixed_half, preferred_element_type=jnp.float32)
    return (passed, part_project, part_output)

def reference(section_inputs, arriving, top_grads, project_weights, output_weights):
    section_count = section_inputs.shape[0]
    tick_count = section_inputs.shape[1]
    width = section_inputs.shape[3]
    project_width = project_weights.shape[2]
    output_width = output_weights.shape[2]
    tick_step = jax.vmap(section_tick)

    def per_replica(totals, replica):
        offset = (replica * SEQ).astype(jnp.int32)
        inputs = lax.dynamic_slice_in_dim(section_inputs, offset, SEQ, 2)
        incoming = lax.dynamic_slice_in_dim(arriving, offset, SEQ, 1)
        later_grads = lax.dynamic_slice_in_dim(top_grads, offset, SEQ, 1)
        sum_project = jnp.zeros((section_count, width, project_width), jnp.float32)
        sum_output = jnp.zeros((section_count, width, output_width), jnp.float32)
        passed = incoming
        for tick_index in range(tick_count):
            passed, part_project, part_output = tick_step(inputs[:, tick_index], incoming, project_weights, output_weights)
            sum_project = sum_project + part_project
            sum_output = sum_output + part_output
            if tick_index + 1 < tick_count:
                incoming = jnp.concatenate([passed[1:], later_grads[tick_index][None]], axis=0)
        rounded_project = lax.optimization_barrier(sum_project.astype(jnp.bfloat16))
        rounded_output = lax.optimization_barrier(sum_output.astype(jnp.bfloat16))
        new_totals = (totals[0] + rounded_project.astype(jnp.float32), totals[1] + rounded_output.astype(jnp.float32))
        return (new_totals, passed)
    start_totals = (jnp.zeros((section_count, width, project_width), jnp.float32), jnp.zeros((section_count, width, output_width), jnp.float32))
    totals, passed_all = lax.scan(per_replica, start_totals, jnp.arange(N_DP, dtype=jnp.int32))
    passed_back = jnp.transpose(passed_all, (1, 0, 2, 3)).reshape(section_count, N_DP * SEQ, width)
    return (totals[0], totals[1], passed_back)
```

```python
import functools
import math

import jax
import jax.numpy as jnp
from jax import lax
from jax.experimental import pallas as pl
from jax.experimental.pallas import tpu as pltpu
from jax.sharding import Mesh
from jax.sharding import PartitionSpec as P

DP = ("dp_0", "dp_1")
MESH = pl.DeviceIdType.MESH
EPSILON = 1e-06
PARTS = 8
ROW_GROUP = 16
CONTRACT_FIRST = (((0,), (0,)), ((), ()))
CONTRACT_LAST = (((1,), (1,)), ((), ()))


def normalize(values):
    centered = values - jnp.mean(values, axis=-1, keepdims=True)
    inverse = lax.rsqrt(jnp.mean(centered * centered, axis=-1, keepdims=True) + EPSILON)
    return (centered * inverse, inverse)


def norm_back(gradient, normed, inverse):
    centered = gradient - jnp.mean(gradient, axis=-1, keepdims=True)
    return inverse * (centered - normed * jnp.mean(gradient * normed, axis=-1, keepdims=True))


def dot32(a, b, dims=None):
    if dims is None:
        return jnp.dot(a, b, preferred_element_type=jnp.float32)
    return lax.dot_general(a, b, dims, preferred_element_type=jnp.float32)


def kernel(
    dims,
    xin,
    arr,
    top,
    wp,
    wo,
    pg_out,
    og_out,
    pass_out,
    xs,
    normed,
    inverse,
    hid,
    hid_t,
    inc,
    inc_t,
    topv,
    full,
    proj_sum,
    head_sum,
    hg,
    sent_back,
    proj_grad,
    mixed,
    part,
    x_relay,
    x_final,
    z_send,
    z_relay,
    z_final,
    own,
    load_sem,
    gather_sem,
    gz_sem,
    gx_sem,
    top_recv,
    top_send,
    pass_recv,
    pass_send,
    xr_sem,
    xf_sem,
    zr_sem,
    zf_sem,
    sx_sem,
    sz_sem,
):
    n_pipe, n_x, n_z, ticks, seq, width, head = dims
    parts, half = PARTS, PARTS // 2
    rows = ticks * seq
    block = width // (n_x * n_z)
    piece = block // parts
    wide = 4 * head
    pw = 3 * head
    root = math.sqrt(head)
    p = lax.axis_index("pipe")
    x = lax.axis_index("dp_0")
    z = lax.axis_index("dp_1")
    x_next, x_prev, x_far = (lax.rem(x + s, n_x) for s in (1, n_x - 1, 2))
    z_next, z_prev, z_far = (lax.rem(z + s, n_z) for s in (1, n_z - 1, 2))
    last = p == n_pipe - 1
    to_x_next, to_x_prev = ({"dp_0": x_next}, {"dp_0": x_prev})
    to_z_next, to_z_prev = ({"dp_1": z_next}, {"dp_1": z_prev})
    pending = []

    def send(src, dst, send_sem, recv_sem, device):
        copy = pltpu.make_async_remote_copy(
            src_ref=src,
            dst_ref=dst,
            send_sem=send_sem,
            recv_sem=recv_sem,
            device_id=device,
            device_id_type=MESH,
        )
        copy.start()
        pending.append(copy)

    def arrived(dst, recv_sem):
        pltpu.make_async_remote_copy(
            src_ref=dst,
            dst_ref=dst,
            send_sem=recv_sem,
            recv_sem=recv_sem,
            device_id=to_x_next,
            device_id_type=MESH,
        ).wait_recv()

    def drain():
        for copy in pending:
            copy.wait_send()
        pending.clear()

    me = x * n_z + z
    loads = [
        pltpu.make_async_copy(xin, xs, load_sem.at[0]),
        pltpu.make_async_copy(wp, full.at[me, :, pl.ds(0, pw)], load_sem.at[1]),
        pltpu.make_async_copy(wo, full.at[me, :, pl.ds(pw, head)], load_sem.at[2]),
        pltpu.make_async_copy(arr, inc.at[pl.ds(0, seq)], load_sem.at[3]),
        pltpu.make_async_copy(top, topv, load_sem.at[4]),
    ]
    for load in loads:
        load.start()

    barrier = pltpu.get_barrier_semaphore()
    for device in (to_x_next, to_x_prev, to_z_next, to_z_prev):
        pl.semaphore_signal(barrier, inc=1, device_id=device, device_id_type=MESH)

    @pl.when(p > 0)
    def _():
        pl.semaphore_signal(barrier, inc=1, device_id={"pipe": p - 1}, device_id_type=MESH)

    @pl.when(p < n_pipe - 1)
    def _():
        pl.semaphore_signal(barrier, inc=1, device_id={"pipe": p + 1}, device_id_type=MESH)
        pl.semaphore_signal(barrier, inc=1, device_id={"pipe": n_pipe - 1}, device_id_type=MESH)

    @pl.when(last)
    def _():
        def greet(i, carry):
            pl.semaphore_signal(barrier, inc=1, device_id={"pipe": i}, device_id_type=MESH)
            return carry

        lax.fori_loop(0, n_pipe - 1, greet, 0)

    loads[0].wait()

    def norm_rows(g, carry):
        at = pl.ds(pl.multiple_of(g * ROW_GROUP, ROW_GROUP), ROW_GROUP)
        values, scale = normalize(xs[at, :].astype(jnp.float32))
        normed[at, :] = values
        hid[at, :] = values.astype(jnp.bfloat16)
        inverse[at, :] = jnp.broadcast_to(scale, (ROW_GROUP, 128))
        return carry

    lax.fori_loop(0, rows // ROW_GROUP, norm_rows, 0)
    for load in loads[1:]:
        load.wait()
    from_neighbours = 4 + jnp.where(p > 0, 1, 0) + jnp.where(last, n_pipe - 1, 2)
    pl.semaphore_wait(barrier, from_neighbours)

    def weight(xx, zz, c):
        return full.at[xx * n_z + zz, pl.ds(c * piece, piece), :]

    def weight_sem(xx, zz, c):
        return gather_sem.at[xx * n_z + zz, c]

    def gather_pair(k):
        phase, j = divmod(k, half)
        za = (z, z_prev, z_next, z_far)[phase]
        zb = (z, z_next, z_prev, z_far)[phase]
        return ((za, j), (zb, half + j))

    def send_weight(xx, at, sem, device):
        zz, c = at
        send(weight(xx, zz, c), weight(xx, zz, c), sem, weight_sem(xx, zz, c), device)

    def weight_arrived(xx, at):
        zz, c = at
        arrived(weight(xx, zz, c), weight_sem(xx, zz, c))

    for j in range(half):
        send_weight(x, (z, j), gz_sem.at[0, j], to_z_next)
        send_weight(x, (z, half + j), gz_sem.at[1, j], to_z_prev)
    for j in range(half):
        send_weight(x, (z, half + j), gz_sem.at[0, half + j], to_z_next)
        send_weight(x, (z, j), gz_sem.at[1, half + j], to_z_prev)

    proj_sum[...] = jnp.zeros_like(proj_sum)
    head_sum[...] = jnp.zeros_like(head_sum)

    def use_block(xx, zz):
        s = xx * n_z + zz
        cols = pl.ds(pl.multiple_of(s * block, block), block)
        proj_sum[...] += dot32(hid[:, cols], full[s, :, :pw])
        head_sum[...] += dot32(inc[:seq, cols], full[s, :, pw:])

    def transpose_block(src, dst, b):
        dst[b * block : (b + 1) * block, :] = src[:, b * block : (b + 1) * block].T

    columns = (x, x_prev, x_next, x_far)
    near = [(xx, z) for xx in columns]
    side = [(xx, zz) for xx in columns for zz in (z_prev, z_next)]
    to_transpose = list(range(n_x * n_z))
    steps = 2 * parts
    for i in range(steps + 3):
        if i < steps:
            a, b = gather_pair(i)
            if i >= half:
                weight_arrived(x, a)
                weight_arrived(x, b)
            if half <= i < parts:
                send_weight(x, a, gz_sem.at[0, i + half], to_z_next)
                send_weight(x, b, gz_sem.at[1, i + half], to_z_prev)
            send_weight(x, a, gx_sem.at[0, i, 0], to_x_next)
            send_weight(x, b, gx_sem.at[1, i, 0], to_x_prev)
            send_weight(x, b, gx_sem.at[0, i, 1], to_x_next)
            send_weight(x, a, gx_sem.at[1, i, 1], to_x_prev)
        if 1 <= i <= steps:
            a, b = gather_pair(i - 1)
            weight_arrived(x_prev, a)
            send_weight(x_prev, a, gx_sem.at[0, i - 1, 2], to_x_next)
            weight_arrived(x_next, b)
            send_weight(x_next, b, gx_sem.at[1, i - 1, 2], to_x_prev)
        if i >= 3:
            a, b = gather_pair(i - 3)
            weight_arrived(x_prev, b)
            weight_arrived(x_next, a)
            weight_arrived(x_far, a)
            weight_arrived(x_far, b)
        if to_transpose:
            transpose_block(hid, hid_t, to_transpose.pop())
        if i > half + 2 and near:
            use_block(*near.pop())
        if i > 3 * half + 2:
            for _ in range(2):
                if side:
                    use_block(*side.pop())
    for b in to_transpose:
        transpose_block(hid, hid_t, b)
    for at in near + side:
        use_block(*at)

    my_cols = pl.ds(pl.multiple_of(p * (width // n_pipe), width // n_pipe), width // n_pipe)
    later = pl.ds(seq, seq)
    top_copy = pltpu.make_async_remote_copy(
        src_ref=topv,
        dst_ref=inc.at[later, my_cols],
        send_sem=top_send,
        recv_sem=top_recv.at[p],
        device_id={"pipe": n_pipe - 1},
        device_id_type=MESH,
    )

    @pl.when(jnp.logical_not(last))
    def _():
        top_copy.start()

    for xx in columns:
        use_block(xx, z_far)

    projected = proj_sum[...]
    query, query_scale = normalize(projected[:, :head])
    key, key_scale = normalize(projected[:, head : 2 * head])
    query_half = query.astype(jnp.bfloat16)
    key_half = key.astype(jnp.bfloat16)
    value_half = projected[:, 2 * head :].astype(jnp.bfloat16)
    attention = []
    for t in range(ticks):
        at = slice(t * seq, (t + 1) * seq)
        powered = jnp.exp(dot32(query_half[at], key_half[at], CONTRACT_LAST) / root)
        attention.append(powered / jnp.sum(powered, axis=-1, keepdims=True))
    attention_half = [a.astype(jnp.bfloat16) for a in attention]

    def head_back(t, head_grad):
        at = slice(t * seq, (t + 1) * seq)
        prob_grad = dot32(head_grad, value_half[at], CONTRACT_LAST)
        value_grad = dot32(attention_half[t], head_grad, CONTRACT_FIRST)
        weighted = attention[t]
        score_grad = (
            weighted
            * (prob_grad - jnp.sum(weighted * prob_grad, axis=-1, keepdims=True))
            / root
        ).astype(jnp.bfloat16)
        query_grad = dot32(score_grad, key_half[at])
        key_grad = dot32(score_grad, query_half[at], CONTRACT_FIRST)
        proj_grad[at, :head] = norm_back(query_grad, query[at], query_scale[at]).astype(
            jnp.bfloat16
        )
        proj_grad[at, head : 2 * head] = norm_back(key_grad, key[at], key_scale[at]).astype(
            jnp.bfloat16
        )
        proj_grad[at, 2 * head :] = value_grad.astype(jnp.bfloat16)

    def hidden_back(t, s):
        hg[:, s * block : (s + 1) * block] = dot32(
            proj_grad[t * seq : (t + 1) * seq, :], full[s, :, :pw], CONTRACT_LAST
        )

    def rows_back(t, g):
        at = slice(g * ROW_GROUP, (g + 1) * ROW_GROUP)
        both = slice(t * seq + g * ROW_GROUP, t * seq + (g + 1) * ROW_GROUP)
        grad = norm_back(hg[at, :], normed[both, :], inverse[both, :1])
        return (inc[both, :].astype(jnp.float32) + grad).astype(jnp.bfloat16)

    head_back(0, head_sum[...].astype(jnp.bfloat16))
    for s in range(n_x * n_z):
        hidden_back(0, s)
    groups = seq // ROW_GROUP
    back_copies = []
    for g in range(groups):
        at = pl.ds(g * ROW_GROUP, ROW_GROUP)
        sent_back[g * ROW_GROUP : (g + 1) * ROW_GROUP, :] = rows_back(0, g)
        back = pltpu.make_async_remote_copy(
            src_ref=sent_back.at[at],
            dst_ref=inc.at[pl.ds(seq + g * ROW_GROUP, ROW_GROUP)],
            send_sem=pass_send.at[g],
            recv_sem=pass_recv.at[g],
            device_id={"pipe": jnp.maximum(p - 1, 0)},
            device_id_type=MESH,
        )
        back_copies.append(back)

        @pl.when(p > 0)
        def _():
            back.start()

    for t in range(ticks):
        at = slice(t * seq, (t + 1) * seq)
        mixed[at, :] = dot32(attention_half[t], value_half[at]).astype(jnp.bfloat16)
    drain()

    @pl.when(last)
    def _():
        top_width = width // n_pipe
        inc[seq:, (n_pipe - 1) * top_width :] = topv[...]

        def one(i, carry):
            cols = pl.ds(pl.multiple_of(i * top_width, top_width), top_width)
            arrived(inc.at[later, cols], top_recv.at[i])
            return carry

        lax.fori_loop(0, n_pipe - 1, one, 0)

    @pl.when(jnp.logical_not(last))
    def _():
        for g in range(groups):
            arrived(inc.at[pl.ds(seq + g * ROW_GROUP, ROW_GROUP)], pass_recv.at[g])

    head_grad = jnp.zeros((seq, head), jnp.float32)
    for s in range(n_x * n_z):
        head_grad += dot32(inc[seq:, s * block : (s + 1) * block], full[s, :, pw:])
        transpose_block(inc, inc_t, s)
    head_back(1, head_grad.astype(jnp.bfloat16))

    def scatter_pair(k):
        phase, j = divmod(k, half)
        za = (z_far, z_prev, z_next, z)[phase]
        zb = (z_far, z_next, z_prev, z)[phase]
        return ((za, j), (zb, half + j))

    around = (x, x_next, x_far, x_prev)
    OWN, NEXT, FAR, PREV = range(4)

    def make_parts(k):
        pieces = []
        for xx in around:
            for zz, c in scatter_pair(k):
                start = (xx * n_z + zz) * block + c * piece
                pieces.append(pl.ds(pl.multiple_of(start, piece), piece))
        projects = dot32(jnp.concatenate([hid_t[at, :] for at in pieces], axis=0), proj_grad[...])
        outputs = dot32(jnp.concatenate([inc_t[at, :] for at in pieces], axis=0), mixed[...])
        for n in range(len(pieces)):
            at = slice(n * piece, (n + 1) * piece)
            part[k, n // 2, n % 2, :, :pw] = projects[at].astype(jnp.bfloat16)
            part[k, n // 2, n % 2, :, pw:] = outputs[at].astype(jnp.bfloat16)

    def added(k, place, ab, relay):
        total = part[k, place, ab].astype(jnp.float32) + relay[...].astype(jnp.float32)
        part[k, place, ab] = total.astype(jnp.bfloat16)

    left, right, hidden_at = 0, 1, 0
    for i in range(steps + 3):
        if i < steps:
            make_parts(i)
            send(part.at[i, FAR, 0], x_relay.at[i, 0], sx_sem.at[i, 0], xr_sem.at[i, 0], to_x_next)
            send(part.at[i, FAR, 1], x_relay.at[i, 1], sx_sem.at[i, 1], xr_sem.at[i, 1], to_x_prev)
            send(
                part.at[i, NEXT, 1],
                x_final.at[i, left, 1],
                sx_sem.at[i, 2],
                xf_sem.at[i, left, 1],
                to_x_next,
            )
            send(
                part.at[i, PREV, 0],
                x_final.at[i, right, 0],
                sx_sem.at[i, 3],
                xf_sem.at[i, right, 0],
                to_x_prev,
            )
        if 1 <= i <= steps:
            k = i - 1
            arrived(x_relay.at[k, 0], xr_sem.at[k, 0])
            added(k, NEXT, 0, x_relay.at[k, 0])
            send(
                part.at[k, NEXT, 0],
                x_final.at[k, left, 0],
                sx_sem.at[k, 4],
                xf_sem.at[k, left, 0],
                to_x_next,
            )
            arrived(x_relay.at[k, 1], xr_sem.at[k, 1])
            added(k, PREV, 1, x_relay.at[k, 1])
            send(
                part.at[k, PREV, 1],
                x_final.at[k, right, 1],
                sx_sem.at[k, 5],
                xf_sem.at[k, right, 1],
                to_x_prev,
            )
        if i >= 3:
            k = i - 3
            phase, j = divmod(k, half)
            for ab in range(2):
                for way in (left, right):
                    arrived(x_final.at[k, way, ab], xf_sem.at[k, way, ab])
                total = (
                    part[k, OWN, ab].astype(jnp.float32)
                    + x_final[k, left, ab].astype(jnp.float32)
                    + x_final[k, right, ab].astype(jnp.float32)
                )
                if phase == 3:
                    own[half * ab + j] = total
                    continue
                if phase == 2:
                    arrived(z_relay.at[j, ab], zr_sem.at[j, ab])
                    total = total + z_relay[j, ab].astype(jnp.float32)
                z_send[k, ab] = total.astype(jnp.bfloat16)
                onward = ab == (1 if phase == 1 else 0)
                device = to_z_next if onward else to_z_prev
                if phase == 0:
                    send(
                        z_send.at[k, ab],
                        z_relay.at[j, ab],
                        sz_sem.at[k, ab],
                        zr_sem.at[j, ab],
                        device,
                    )
                else:
                    way, c = (left if onward else right, half * ab + j)
                    send(
                        z_send.at[k, ab],
                        z_final.at[way, c],
                        sz_sem.at[k, ab],
                        zf_sem.at[way, c],
                        device,
                    )
        if hidden_at < n_x * n_z:
            hidden_back(1, hidden_at)
            hidden_at += 1
    for s in range(hidden_at, n_x * n_z):
        hidden_back(1, s)
    for g in range(groups):
        pass_out[g * ROW_GROUP : (g + 1) * ROW_GROUP, :] = rows_back(1, g)
    for ab in (1, 0):
        for j in range(half):
            c = half * ab + j
            arrived(z_final.at[left, c], zf_sem.at[left, c])
            arrived(z_final.at[right, c], zf_sem.at[right, c])
            total = (
                own[c]
                + z_final[left, c].astype(jnp.float32)
                + z_final[right, c].astype(jnp.float32)
            )
            pg_out[c * piece : (c + 1) * piece, :] = total[:, :pw]
            og_out[c * piece : (c + 1) * piece, :] = total[:, pw:]
    drain()

    @pl.when(p > 0)
    def _():
        for back in back_copies:
            back.wait_send()

    @pl.when(jnp.logical_not(last))
    def _():
        top_copy.wait_send()


def shards(n_pipe, n_x, n_z, section_inputs, arriving, top_grads, project_weights, output_weights):
    _, ticks, seq, width = section_inputs.shape
    head = output_weights.shape[2]
    rows = ticks * seq
    block = width // (n_x * n_z)
    piece = block // PARTS
    half, steps, wide = PARTS // 2, 2 * PARTS, 4 * head
    low, high = jnp.bfloat16, jnp.float32
    dma = pltpu.SemaphoreType.DMA
    scratch = [
        pltpu.VMEM((rows, width), low),
        pltpu.VMEM((rows, width), high),
        pltpu.VMEM((rows, 128), high),
        pltpu.VMEM((rows, width), low),
        pltpu.VMEM((width, rows), low),
        pltpu.VMEM((rows, width), low),
        pltpu.VMEM((width, rows), low),
        pltpu.VMEM((seq, width // n_pipe), low),
        pltpu.VMEM((n_x * n_z, block, wide), low),
        pltpu.VMEM((rows, 3 * head), high),
        pltpu.VMEM((seq, head), high),
        pltpu.VMEM((seq, width), high),
        pltpu.VMEM((seq, width), low),
        pltpu.VMEM((rows, 3 * head), low),
        pltpu.VMEM((rows, head), low),
        pltpu.VMEM((steps, 4, 2, piece, wide), low),
        pltpu.VMEM((steps, 2, piece, wide), low),
        pltpu.VMEM((steps, 2, 2, piece, wide), low),
        pltpu.VMEM((3 * half, 2, piece, wide), low),
        pltpu.VMEM((half, 2, piece, wide), low),
        pltpu.VMEM((2, PARTS, piece, wide), low),
        pltpu.VMEM((PARTS, piece, wide), high),
        dma((5,)),
        dma((n_x * n_z, PARTS)),
        dma((2, 3 * half)),
        dma((2, steps, 3)),
        dma((n_pipe,)),
        dma(()),
        dma((seq // ROW_GROUP,)),
        dma((seq // ROW_GROUP,)),
        dma((steps, 2)),
        dma((steps, 2, 2)),
        dma((half, 2)),
        dma((2, PARTS)),
        dma((steps, 6)),
        dma((3 * half, 2)),
    ]
    anywhere = pl.BlockSpec(memory_space=pl.ANY)
    project, output, passed = pl.pallas_call(
        functools.partial(kernel, (n_pipe, n_x, n_z, ticks, seq, width, head)),
        out_shape=(
            jax.ShapeDtypeStruct((block, 3 * head), high),
            jax.ShapeDtypeStruct((block, head), high),
            jax.ShapeDtypeStruct((seq, width), low),
        ),
        in_specs=[anywhere] * 5,
        out_specs=[pl.BlockSpec(memory_space=pltpu.VMEM)] * 3,
        scratch_shapes=scratch,
        compiler_params=pltpu.CompilerParams(
            collective_id=0, has_side_effects=True, vmem_limit_bytes=60 * 1024 * 1024
        ),
    )(
        section_inputs.reshape(rows, width),
        arriving[0],
        top_grads[0],
        project_weights[0],
        output_weights[0],
    )
    return (project[None], output[None], passed[None])


def solution(mesh):
    n_x = n_z = 4
    split = Mesh(mesh.devices.reshape(mesh.shape["pipe"], n_x, n_z), ("pipe", "dp_0", "dp_1"))
    in_specs = (
        P("pipe", None, DP, None),
        P("pipe", DP, None),
        P(None, DP, "pipe"),
        P("pipe", DP, None),
        P("pipe", DP, None),
    )
    out_specs = (P("pipe", DP, None), P("pipe", DP, None), P("pipe", DP, None))
    return jax.shard_map(
        functools.partial(shards, mesh.shape["pipe"], n_x, n_z),
        mesh=split,
        in_specs=in_specs,
        out_specs=out_specs,
        check_vma=False,
    )
```

```python
import functools
import math

import jax
import jax.numpy as jnp
from jax import lax
from jax.experimental import pallas as pl
from jax.experimental.pallas import tpu as pltpu
from jax.sharding import Mesh
from jax.sharding import PartitionSpec as P

DP = ("dp_0", "dp_1")
MESH = pl.DeviceIdType.MESH
EPSILON = 1e-06
PARTS = 8
SLOW_WINDOW = 2
ROW_GROUP = 16
CONTRACT_FIRST = (((0,), (0,)), ((), ()))
CONTRACT_LAST = (((1,), (1,)), ((), ()))


def normalize(values):
    centered = values - jnp.mean(values, axis=-1, keepdims=True)
    inverse = lax.rsqrt(jnp.mean(centered * centered, axis=-1, keepdims=True) + EPSILON)
    return (centered * inverse, inverse)


def norm_back(gradient, normed, inverse):
    centered = gradient - jnp.mean(gradient, axis=-1, keepdims=True)
    return inverse * (centered - normed * jnp.mean(gradient * normed, axis=-1, keepdims=True))


def dot32(a, b, dims=None):
    if dims is None:
        return jnp.dot(a, b, preferred_element_type=jnp.float32)
    return lax.dot_general(a, b, dims, preferred_element_type=jnp.float32)


def kernel(
    dims,
    xin,
    arr,
    top,
    wp,
    wo,
    pg_out,
    og_out,
    pass_out,
    xs,
    normed,
    inverse,
    hid,
    hid_t,
    inc,
    inc_t,
    topv,
    full,
    proj_sum,
    head_sum,
    hg,
    sent_back,
    proj_grad,
    mixed,
    part,
    x_relay,
    x_final,
    z_send,
    z_relay,
    z_final,
    own,
    load_sem,
    gather_sem,
    gz_sem,
    gx_sem,
    top_recv,
    top_send,
    pass_recv,
    pass_send,
    xr_sem,
    xf_sem,
    zr_sem,
    zf_sem,
    sx_sem,
    sz_sem,
):
    n_pipe, n_x, n_z, ticks, seq, width, head = dims
    parts, half = PARTS, PARTS // 2
    rows = ticks * seq
    block = width // (n_x * n_z)
    piece = block // parts
    wide = 4 * head
    pw = 3 * head
    root = math.sqrt(head)
    p = lax.axis_index("pipe")
    x = lax.axis_index("dp_0")
    z = lax.axis_index("dp_1")
    x_next, x_prev, x_far = (lax.rem(x + s, n_x) for s in (1, n_x - 1, 2))
    z_next, z_prev, z_far = (lax.rem(z + s, n_z) for s in (1, n_z - 1, 2))
    last = p == n_pipe - 1
    to_x_next, to_x_prev = ({"dp_0": x_next}, {"dp_0": x_prev})
    to_z_next, to_z_prev = ({"dp_1": z_next}, {"dp_1": z_prev})
    pending = []

    def send(src, dst, send_sem, recv_sem, device, keep=True):
        copy = pltpu.make_async_remote_copy(
            src_ref=src,
            dst_ref=dst,
            send_sem=send_sem,
            recv_sem=recv_sem,
            device_id=device,
            device_id_type=MESH,
        )
        copy.start()
        if keep:
            pending.append(copy)

    def arrived(dst, recv_sem):
        pltpu.make_async_remote_copy(
            src_ref=dst,
            dst_ref=dst,
            send_sem=recv_sem,
            recv_sem=recv_sem,
            device_id=to_x_next,
            device_id_type=MESH,
        ).wait_recv()

    def sent(src, send_sem):
        pltpu.make_async_remote_copy(
            src_ref=src,
            dst_ref=src,
            send_sem=send_sem,
            recv_sem=send_sem,
            device_id=to_x_next,
            device_id_type=MESH,
        ).wait_send()

    def drain():
        for copy in pending:
            copy.wait_send()
        pending.clear()

    me = x * n_z + z
    loads = [
        pltpu.make_async_copy(wp, full.at[me, :, pl.ds(0, pw)], load_sem.at[0]),
        pltpu.make_async_copy(wo, full.at[me, :, pl.ds(pw, head)], load_sem.at[1]),
        pltpu.make_async_copy(xin, xs, load_sem.at[2]),
        pltpu.make_async_copy(arr, inc.at[pl.ds(0, seq)], load_sem.at[3]),
        pltpu.make_async_copy(top, topv, load_sem.at[4]),
    ]
    for load in loads:
        load.start()

    barrier = pltpu.get_barrier_semaphore()
    for device in (to_x_next, to_x_prev, to_z_next, to_z_prev):
        pl.semaphore_signal(barrier, inc=1, device_id=device, device_id_type=MESH)

    @pl.when(p > 0)
    def _():
        pl.semaphore_signal(barrier, inc=1, device_id={"pipe": p - 1}, device_id_type=MESH)

    @pl.when(p < n_pipe - 1)
    def _():
        pl.semaphore_signal(barrier, inc=1, device_id={"pipe": p + 1}, device_id_type=MESH)
        pl.semaphore_signal(barrier, inc=1, device_id={"pipe": n_pipe - 1}, device_id_type=MESH)

    @pl.when(last)
    def _():
        def greet(i, carry):
            pl.semaphore_signal(barrier, inc=1, device_id={"pipe": i}, device_id_type=MESH)
            return carry

        lax.fori_loop(0, n_pipe - 1, greet, 0)

    loads[0].wait()
    loads[1].wait()
    from_neighbours = 4 + jnp.where(p > 0, 1, 0) + jnp.where(last, n_pipe - 1, 2)
    pl.semaphore_wait(barrier, from_neighbours)

    def weight(xx, zz, c):
        return full.at[xx * n_z + zz, pl.ds(c * piece, piece), :]

    def weight_sem(xx, zz, c):
        return gather_sem.at[xx * n_z + zz, c]

    def gather_pair(k):
        phase, j = divmod(k, half)
        za = (z, z_prev, z_next, z_far)[phase]
        zb = (z, z_next, z_prev, z_far)[phase]
        return ((za, j), (zb, half + j))

    def send_weight(xx, at, sem, device, keep=True):
        zz, c = at
        send(weight(xx, zz, c), weight(xx, zz, c), sem, weight_sem(xx, zz, c), device, keep)

    def weight_arrived(xx, at):
        zz, c = at
        arrived(weight(xx, zz, c), weight_sem(xx, zz, c))

    ahead = lax.rem(p, 2) == 0
    n_items = parts + half

    def z_item(n):
        if n < half:
            up, down = (z, n), (z, half + n)
        elif n < parts:
            up, down = (z, n), (z, n - half)
        else:
            up, down = gather_pair(half + n - parts)
        send_weight(x, up, gz_sem.at[0, n], to_z_next, False)
        send_weight(x, down, gz_sem.at[1, n], to_z_prev, False)

    def z_items(first, slow_first, count, slow_count):
        @pl.when(ahead)
        def _():
            for n in range(first, min(first + count, n_items)):
                z_item(n)

        @pl.when(jnp.logical_not(ahead))
        def _():
            for n in range(slow_first, min(slow_first + slow_count, n_items)):
                z_item(n)

    z_items(0, 0, parts, SLOW_WINDOW)

    def share_pair(i):
        a, b = gather_pair(i)
        send_weight(x, a, gx_sem.at[0, i, 0], to_x_next)
        send_weight(x, b, gx_sem.at[1, i, 0], to_x_prev)
        send_weight(x, b, gx_sem.at[0, i, 1], to_x_next)
        send_weight(x, a, gx_sem.at[1, i, 1], to_x_prev)

    for i in range(half):
        share_pair(i)

    loads[2].wait()

    def norm_rows(g, carry):
        at = pl.ds(pl.multiple_of(g * ROW_GROUP, ROW_GROUP), ROW_GROUP)
        values, scale = normalize(xs[at, :].astype(jnp.float32))
        normed[at, :] = values
        hid[at, :] = values.astype(jnp.bfloat16)
        inverse[at, :] = jnp.broadcast_to(scale, (ROW_GROUP, 128))
        return carry

    lax.fori_loop(0, rows // ROW_GROUP, norm_rows, 0)
    for load in loads[3:]:
        load.wait()

    proj_sum[...] = jnp.zeros_like(proj_sum)
    head_sum[...] = jnp.zeros_like(head_sum)

    def use_blocks(places):
        project, output = 0.0, 0.0
        for xx, zz in places:
            s = xx * n_z + zz
            cols = pl.ds(pl.multiple_of(s * block, block), block)
            project += dot32(hid[:, cols], full[s, :, :pw])
            output += dot32(inc[:seq, cols], full[s, :, pw:])
        proj_sum[...] += project
        head_sum[...] += output

    def transpose_block(src, dst, b):
        dst[b * block : (b + 1) * block, :] = src[:, b * block : (b + 1) * block].T

    columns = (x, x_prev, x_next, x_far)
    steps = 2 * parts
    for i in range(steps + 3):
        if i < steps:
            a, b = gather_pair(i)
            if i >= half:
                weight_arrived(x, a)
                weight_arrived(x, b)
                z_items(parts + i - half, SLOW_WINDOW + i - half, 1, 1)
                share_pair(i)
        if 1 <= i <= steps:
            a, b = gather_pair(i - 1)
            weight_arrived(x_prev, a)
            send_weight(x_prev, a, gx_sem.at[0, i - 1, 2], to_x_next)
            weight_arrived(x_next, b)
            send_weight(x_next, b, gx_sem.at[1, i - 1, 2], to_x_prev)
        if i >= 3:
            a, b = gather_pair(i - 3)
            weight_arrived(x_prev, b)
            weight_arrived(x_next, a)
            weight_arrived(x_far, a)
            weight_arrived(x_far, b)
        if 1 <= i <= parts:
            for b in range(2 * i - 2, 2 * i):
                transpose_block(hid, hid_t, b)
        if i == half + 2:
            use_blocks([(xx, z) for xx in columns])
        if i == 3 * half + 2:
            use_blocks([(xx, zz) for xx in columns for zz in (z_prev, z_next)])
        if i == steps:
            use_blocks([(x, z_far)])

    my_cols = pl.ds(pl.multiple_of(p * (width // n_pipe), width // n_pipe), width // n_pipe)
    later = pl.ds(seq, seq)
    top_copy = pltpu.make_async_remote_copy(
        src_ref=topv,
        dst_ref=inc.at[later, my_cols],
        send_sem=top_send,
        recv_sem=top_recv.at[p],
        device_id={"pipe": n_pipe - 1},
        device_id_type=MESH,
    )

    @pl.when(jnp.logical_not(last))
    def _():
        top_copy.start()

    use_blocks([(xx, z_far) for xx in (x_prev, x_next, x_far)])

    projected = proj_sum[...]
    query, query_scale = normalize(projected[:, :head])
    key, key_scale = normalize(projected[:, head : 2 * head])
    query_half = query.astype(jnp.bfloat16)
    key_half = key.astype(jnp.bfloat16)
    value_half = projected[:, 2 * head :].astype(jnp.bfloat16)
    attention = []
    for t in range(ticks):
        at = slice(t * seq, (t + 1) * seq)
        powered = jnp.exp(dot32(query_half[at], key_half[at], CONTRACT_LAST) / root)
        attention.append(powered / jnp.sum(powered, axis=-1, keepdims=True))
    attention_half = [a.astype(jnp.bfloat16) for a in attention]

    def head_back(t, head_grad):
        at = slice(t * seq, (t + 1) * seq)
        prob_grad = dot32(head_grad, value_half[at], CONTRACT_LAST)
        value_grad = dot32(attention_half[t], head_grad, CONTRACT_FIRST)
        weighted = attention[t]
        score_grad = (
            weighted
            * (prob_grad - jnp.sum(weighted * prob_grad, axis=-1, keepdims=True))
            / root
        ).astype(jnp.bfloat16)
        query_grad = dot32(score_grad, key_half[at])
        key_grad = dot32(score_grad, query_half[at], CONTRACT_FIRST)
        proj_grad[at, :head] = norm_back(query_grad, query[at], query_scale[at]).astype(
            jnp.bfloat16
        )
        proj_grad[at, head : 2 * head] = norm_back(key_grad, key[at], key_scale[at]).astype(
            jnp.bfloat16
        )
        proj_grad[at, 2 * head :] = value_grad.astype(jnp.bfloat16)

    def hidden_back(t, s):
        hg[:, s * block : (s + 1) * block] = dot32(
            proj_grad[t * seq : (t + 1) * seq, :], full[s, :, :pw], CONTRACT_LAST
        )

    def rows_back(t, g):
        at = slice(g * ROW_GROUP, (g + 1) * ROW_GROUP)
        both = slice(t * seq + g * ROW_GROUP, t * seq + (g + 1) * ROW_GROUP)
        grad = norm_back(hg[at, :], normed[both, :], inverse[both, :1])
        return (inc[both, :].astype(jnp.float32) + grad).astype(jnp.bfloat16)

    head_back(0, head_sum[...].astype(jnp.bfloat16))
    for s in range(n_x * n_z):
        hidden_back(0, s)
    groups = seq // ROW_GROUP
    back_copies = []
    for g in range(groups):
        at = pl.ds(g * ROW_GROUP, ROW_GROUP)
        sent_back[g * ROW_GROUP : (g + 1) * ROW_GROUP, :] = rows_back(0, g)
        back = pltpu.make_async_remote_copy(
            src_ref=sent_back.at[at],
            dst_ref=inc.at[pl.ds(seq + g * ROW_GROUP, ROW_GROUP)],
            send_sem=pass_send.at[g],
            recv_sem=pass_recv.at[g],
            device_id={"pipe": jnp.maximum(p - 1, 0)},
            device_id_type=MESH,
        )
        back_copies.append(back)

        @pl.when(p > 0)
        def _():
            back.start()

    for t in range(ticks):
        at = slice(t * seq, (t + 1) * seq)
        mixed[at, :] = dot32(attention_half[t], value_half[at]).astype(jnp.bfloat16)
    drain()
    for n in range(n_items):
        for way in range(2):
            sent(weight(x, z, 0), gz_sem.at[way, n])

    @pl.when(last)
    def _():
        top_width = width // n_pipe
        inc[seq:, (n_pipe - 1) * top_width :] = topv[...]

        def one(i, carry):
            cols = pl.ds(pl.multiple_of(i * top_width, top_width), top_width)
            arrived(inc.at[later, cols], top_recv.at[i])
            return carry

        lax.fori_loop(0, n_pipe - 1, one, 0)

    @pl.when(jnp.logical_not(last))
    def _():
        for g in range(groups):
            arrived(inc.at[pl.ds(seq + g * ROW_GROUP, ROW_GROUP)], pass_recv.at[g])

    head_grad = jnp.zeros((seq, head), jnp.float32)
    for s in range(n_x * n_z):
        head_grad += dot32(inc[seq:, s * block : (s + 1) * block], full[s, :, pw:])
        transpose_block(inc, inc_t, s)
    head_back(1, head_grad.astype(jnp.bfloat16))

    def scatter_pair(k):
        phase, j = divmod(k, half)
        za = (z_far, z_prev, z_next, z)[phase]
        zb = (z_far, z_next, z_prev, z)[phase]
        return ((za, j), (zb, half + j))

    around = (x, x_next, x_far, x_prev)
    OWN, NEXT, FAR, PREV = range(4)

    def make_parts(k):
        pieces = []
        for xx in around:
            for zz, c in scatter_pair(k):
                start = (xx * n_z + zz) * block + c * piece
                pieces.append(pl.ds(pl.multiple_of(start, piece), piece))
        projects = dot32(jnp.concatenate([hid_t[at, :] for at in pieces], axis=0), proj_grad[...])
        outputs = dot32(jnp.concatenate([inc_t[at, :] for at in pieces], axis=0), mixed[...])
        for n in range(len(pieces)):
            at = slice(n * piece, (n + 1) * piece)
            part[k, n // 2, n % 2, :, :pw] = projects[at].astype(jnp.bfloat16)
            part[k, n // 2, n % 2, :, pw:] = outputs[at].astype(jnp.bfloat16)

    def added(k, place, ab, relay):
        total = part[k, place, ab].astype(jnp.float32) + relay[...].astype(jnp.float32)
        part[k, place, ab] = total.astype(jnp.bfloat16)

    left, right, hidden_at = 0, 1, 0
    for i in range(steps + 3):
        if i < steps:
            make_parts(i)
            send(part.at[i, FAR, 0], x_relay.at[i, 0], sx_sem.at[i, 0], xr_sem.at[i, 0], to_x_next)
            send(part.at[i, FAR, 1], x_relay.at[i, 1], sx_sem.at[i, 1], xr_sem.at[i, 1], to_x_prev)
            send(
                part.at[i, NEXT, 1],
                x_final.at[i, left, 1],
                sx_sem.at[i, 2],
                xf_sem.at[i, left, 1],
                to_x_next,
            )
            send(
                part.at[i, PREV, 0],
                x_final.at[i, right, 0],
                sx_sem.at[i, 3],
                xf_sem.at[i, right, 0],
                to_x_prev,
            )
        if 1 <= i <= steps:
            k = i - 1
            arrived(x_relay.at[k, 0], xr_sem.at[k, 0])
            added(k, NEXT, 0, x_relay.at[k, 0])
            send(
                part.at[k, NEXT, 0],
                x_final.at[k, left, 0],
                sx_sem.at[k, 4],
                xf_sem.at[k, left, 0],
                to_x_next,
            )
            arrived(x_relay.at[k, 1], xr_sem.at[k, 1])
            added(k, PREV, 1, x_relay.at[k, 1])
            send(
                part.at[k, PREV, 1],
                x_final.at[k, right, 1],
                sx_sem.at[k, 5],
                xf_sem.at[k, right, 1],
                to_x_prev,
            )
        if i >= 3:
            k = i - 3
            phase, j = divmod(k, half)
            for ab in range(2):
                for way in (left, right):
                    arrived(x_final.at[k, way, ab], xf_sem.at[k, way, ab])
                total = (
                    part[k, OWN, ab].astype(jnp.float32)
                    + x_final[k, left, ab].astype(jnp.float32)
                    + x_final[k, right, ab].astype(jnp.float32)
                )
                if phase == 3:
                    own[half * ab + j] = total
                    continue
                if phase == 2:
                    arrived(z_relay.at[j, ab], zr_sem.at[j, ab])
                    total = total + z_relay[j, ab].astype(jnp.float32)
                z_send[k, ab] = total.astype(jnp.bfloat16)
                onward = ab == (1 if phase == 1 else 0)
                device = to_z_next if onward else to_z_prev
                if phase == 0:
                    send(
                        z_send.at[k, ab],
                        z_relay.at[j, ab],
                        sz_sem.at[k, ab],
                        zr_sem.at[j, ab],
                        device,
                    )
                else:
                    way, c = (left if onward else right, half * ab + j)
                    send(
                        z_send.at[k, ab],
                        z_final.at[way, c],
                        sz_sem.at[k, ab],
                        zf_sem.at[way, c],
                        device,
                    )
        if hidden_at < n_x * n_z:
            hidden_back(1, hidden_at)
            hidden_at += 1
    for s in range(hidden_at, n_x * n_z):
        hidden_back(1, s)
    for g in range(groups):
        pass_out[g * ROW_GROUP : (g + 1) * ROW_GROUP, :] = rows_back(1, g)
    for ab in (1, 0):
        for j in range(half):
            c = half * ab + j
            arrived(z_final.at[left, c], zf_sem.at[left, c])
            arrived(z_final.at[right, c], zf_sem.at[right, c])
            total = (
                own[c]
                + z_final[left, c].astype(jnp.float32)
                + z_final[right, c].astype(jnp.float32)
            )
            pg_out[c * piece : (c + 1) * piece, :] = total[:, :pw]
            og_out[c * piece : (c + 1) * piece, :] = total[:, pw:]
    drain()

    @pl.when(p > 0)
    def _():
        for back in back_copies:
            back.wait_send()

    @pl.when(jnp.logical_not(last))
    def _():
        top_copy.wait_send()


def put_out(pg_in, og_in, pass_in, pg_out, og_out, pass_out, sems):
    pairs = ((pg_in, pg_out), (og_in, og_out), (pass_in, pass_out))
    copies = [pltpu.make_async_copy(a, b, sems.at[n]) for n, (a, b) in enumerate(pairs)]
    for copy in copies:
        copy.start()
    for copy in copies:
        copy.wait()


def shards(n_pipe, n_x, n_z, section_inputs, arriving, top_grads, project_weights, output_weights):
    _, ticks, seq, width = section_inputs.shape
    head = output_weights.shape[2]
    rows = ticks * seq
    block = width // (n_x * n_z)
    piece = block // PARTS
    half, steps, wide = PARTS // 2, 2 * PARTS, 4 * head
    low, high = jnp.bfloat16, jnp.float32
    dma = pltpu.SemaphoreType.DMA
    scratch = [
        pltpu.VMEM((rows, width), low),
        pltpu.VMEM((rows, width), high),
        pltpu.VMEM((rows, 128), high),
        pltpu.VMEM((rows, width), low),
        pltpu.VMEM((width, rows), low),
        pltpu.VMEM((rows, width), low),
        pltpu.VMEM((width, rows), low),
        pltpu.VMEM((seq, width // n_pipe), low),
        pltpu.VMEM((n_x * n_z, block, wide), low),
        pltpu.VMEM((rows, 3 * head), high),
        pltpu.VMEM((seq, head), high),
        pltpu.VMEM((seq, width), high),
        pltpu.VMEM((seq, width), low),
        pltpu.VMEM((rows, 3 * head), low),
        pltpu.VMEM((rows, head), low),
        pltpu.VMEM((steps, 4, 2, piece, wide), low),
        pltpu.VMEM((steps, 2, piece, wide), low),
        pltpu.VMEM((steps, 2, 2, piece, wide), low),
        pltpu.VMEM((3 * half, 2, piece, wide), low),
        pltpu.VMEM((half, 2, piece, wide), low),
        pltpu.VMEM((2, PARTS, piece, wide), low),
        pltpu.VMEM((PARTS, piece, wide), high),
        dma((5,)),
        dma((n_x * n_z, PARTS)),
        dma((2, 3 * half)),
        dma((2, steps, 3)),
        dma((n_pipe,)),
        dma(()),
        dma((seq // ROW_GROUP,)),
        dma((seq // ROW_GROUP,)),
        dma((steps, 2)),
        dma((steps, 2, 2)),
        dma((half, 2)),
        dma((2, PARTS)),
        dma((steps, 6)),
        dma((3 * half, 2)),
    ]
    anywhere = pl.BlockSpec(memory_space=pl.ANY)
    results = pl.pallas_call(
        functools.partial(kernel, (n_pipe, n_x, n_z, ticks, seq, width, head)),
        out_shape=(
            pltpu.VMEM((block, 3 * head), high),
            pltpu.VMEM((block, head), high),
            pltpu.VMEM((seq, width), low),
        ),
        in_specs=[pl.BlockSpec(memory_space=pltpu.HBM)] * 5,
        out_specs=[pl.BlockSpec(memory_space=pltpu.VMEM)] * 3,
        scratch_shapes=scratch,
        compiler_params=pltpu.CompilerParams(
            collective_id=0, has_side_effects=True, vmem_limit_bytes=65_900_000
        ),
    )(
        section_inputs.reshape(rows, width),
        arriving[0],
        top_grads[0],
        project_weights[0],
        output_weights[0],
    )
    project, output, passed = pl.pallas_call(
        put_out,
        out_shape=(
            jax.ShapeDtypeStruct((block, 3 * head), high),
            jax.ShapeDtypeStruct((block, head), high),
            jax.ShapeDtypeStruct((seq, width), low),
        ),
        in_specs=[pl.BlockSpec(memory_space=pltpu.VMEM)] * 3,
        out_specs=[anywhere] * 3,
        scratch_shapes=[dma((3,))],
        compiler_params=pltpu.CompilerParams(vmem_limit_bytes=4 * 1024 * 1024),
    )(*results)
    return (project[None], output[None], passed[None])


def solution(mesh):
    n_x = n_z = 4
    split = Mesh(mesh.devices.reshape(mesh.shape["pipe"], n_x, n_z), ("pipe", "dp_0", "dp_1"))
    in_specs = (
        P("pipe", None, DP, None),
        P("pipe", DP, None),
        P(None, DP, "pipe"),
        P("pipe", DP, None),
        P("pipe", DP, None),
    )
    out_specs = (P("pipe", DP, None), P("pipe", DP, None), P("pipe", DP, None))
    return jax.shard_map(
        functools.partial(shards, mesh.shape["pipe"], n_x, n_z),
        mesh=split,
        in_specs=in_specs,
        out_specs=out_specs,
        check_vma=False,
    )
```

```python
import functools
import math

import jax
import jax.numpy as jnp
from jax import lax
from jax.experimental import pallas as pl
from jax.experimental.pallas import tpu as pltpu
from jax.sharding import Mesh
from jax.sharding import PartitionSpec as P

DP = ("dp_0", "dp_1")
MESH = pl.DeviceIdType.MESH
EPSILON = 1e-06
PARTS = 8
SLOW_WINDOW = 2
ROW_GROUP = 16
CONTRACT_FIRST = (((0,), (0,)), ((), ()))
CONTRACT_LAST = (((1,), (1,)), ((), ()))


def normalize(values):
    centered = values - jnp.mean(values, axis=-1, keepdims=True)
    inverse = lax.rsqrt(jnp.mean(centered * centered, axis=-1, keepdims=True) + EPSILON)
    return (centered * inverse, inverse)


def norm_back(gradient, normed, inverse):
    centered = gradient - jnp.mean(gradient, axis=-1, keepdims=True)
    return inverse * (centered - normed * jnp.mean(gradient * normed, axis=-1, keepdims=True))


def dot32(a, b, dims=None):
    if dims is None:
        return jnp.dot(a, b, preferred_element_type=jnp.float32)
    return lax.dot_general(a, b, dims, preferred_element_type=jnp.float32)


def kernel(
    dims,
    xin,
    arr,
    top,
    wp,
    wo,
    pg_out,
    og_out,
    pass_out,
    xs,
    normed,
    inverse,
    hid,
    hid_t,
    inc,
    inc_t,
    topv,
    full,
    proj_sum,
    head_sum,
    hg,
    sent_back,
    proj_grad,
    mixed,
    part,
    x_relay,
    x_final,
    z_send,
    z_relay,
    z_final,
    own,
    load_sem,
    gather_sem,
    gz_sem,
    gx_sem,
    top_recv,
    top_send,
    pass_recv,
    pass_send,
    xr_sem,
    xf_sem,
    zr_sem,
    zf_sem,
    sx_sem,
    sz_sem,
    top_ready,
):
    n_pipe, n_x, n_z, ticks, seq, width, head = dims
    parts, half = PARTS, PARTS // 2
    rows = ticks * seq
    block = width // (n_x * n_z)
    piece = block // parts
    wide = 4 * head
    pw = 3 * head
    root = math.sqrt(head)
    p = lax.axis_index("pipe")
    x = lax.axis_index("dp_0")
    z = lax.axis_index("dp_1")
    x_next, x_prev, x_far = (lax.rem(x + s, n_x) for s in (1, n_x - 1, 2))
    z_next, z_prev, z_far = (lax.rem(z + s, n_z) for s in (1, n_z - 1, 2))
    last = p == n_pipe - 1
    to_x_next, to_x_prev = ({"dp_0": x_next}, {"dp_0": x_prev})
    to_z_next, to_z_prev = ({"dp_1": z_next}, {"dp_1": z_prev})
    pending = []

    def send(src, dst, send_sem, recv_sem, device, keep=True):
        copy = pltpu.make_async_remote_copy(
            src_ref=src,
            dst_ref=dst,
            send_sem=send_sem,
            recv_sem=recv_sem,
            device_id=device,
            device_id_type=MESH,
        )
        copy.start()
        if keep:
            pending.append(copy)

    def arrived(dst, recv_sem):
        pltpu.make_async_remote_copy(
            src_ref=dst,
            dst_ref=dst,
            send_sem=recv_sem,
            recv_sem=recv_sem,
            device_id=to_x_next,
            device_id_type=MESH,
        ).wait_recv()

    def sent(src, send_sem):
        pltpu.make_async_remote_copy(
            src_ref=src,
            dst_ref=src,
            send_sem=send_sem,
            recv_sem=send_sem,
            device_id=to_x_next,
            device_id_type=MESH,
        ).wait_send()

    def drain():
        for copy in pending:
            copy.wait_send()
        pending.clear()

    me = x * n_z + z
    loads = [
        pltpu.make_async_copy(wp, full.at[me, :, pl.ds(0, pw)], load_sem.at[0]),
        pltpu.make_async_copy(wo, full.at[me, :, pl.ds(pw, head)], load_sem.at[1]),
        pltpu.make_async_copy(xin, xs, load_sem.at[2]),
        pltpu.make_async_copy(arr, inc.at[pl.ds(0, seq)], load_sem.at[3]),
        pltpu.make_async_copy(top, topv, load_sem.at[4]),
    ]
    for load in loads:
        load.start()

    barrier = pltpu.get_barrier_semaphore()
    for device in (to_x_next, to_x_prev, to_z_next, to_z_prev):
        pl.semaphore_signal(barrier, inc=1, device_id=device, device_id_type=MESH)

    @pl.when(p > 0)
    def _():
        pl.semaphore_signal(barrier, inc=1, device_id={"pipe": p - 1}, device_id_type=MESH)

    @pl.when(p < n_pipe - 1)
    def _():
        pl.semaphore_signal(barrier, inc=1, device_id={"pipe": p + 1}, device_id_type=MESH)
        pl.semaphore_signal(barrier, inc=1, device_id={"pipe": n_pipe - 1}, device_id_type=MESH)

    loads[0].wait()
    loads[1].wait()
    from_neighbours = 4 + jnp.where(p > 0, 1, 0) + jnp.where(last, n_pipe - 1, 1)
    pl.semaphore_wait(barrier, from_neighbours)

    def weight(xx, zz, c):
        return full.at[xx * n_z + zz, pl.ds(c * piece, piece), :]

    def weight_sem(xx, zz, c):
        return gather_sem.at[xx * n_z + zz, c]

    def gather_pair(k):
        phase, j = divmod(k, half)
        za = (z, z_prev, z_next, z_far)[phase]
        zb = (z, z_next, z_prev, z_far)[phase]
        return ((za, j), (zb, half + j))

    def send_weight(xx, at, sem, device, keep=True):
        zz, c = at
        send(weight(xx, zz, c), weight(xx, zz, c), sem, weight_sem(xx, zz, c), device, keep)

    def weight_arrived(xx, at):
        zz, c = at
        arrived(weight(xx, zz, c), weight_sem(xx, zz, c))

    ahead = lax.rem(p, 2) == 0
    n_items = parts + half

    def z_item(n):
        if n < half:
            up, down = (z, n), (z, half + n)
        elif n < parts:
            up, down = (z, n), (z, n - half)
        else:
            up, down = gather_pair(half + n - parts)
        send_weight(x, up, gz_sem.at[0, n], to_z_next, False)
        send_weight(x, down, gz_sem.at[1, n], to_z_prev, False)

    def z_items(first, slow_first, count, slow_count):
        @pl.when(ahead)
        def _():
            for n in range(first, min(first + count, n_items)):
                z_item(n)

        @pl.when(jnp.logical_not(ahead))
        def _():
            for n in range(slow_first, min(slow_first + slow_count, n_items)):
                z_item(n)

    z_items(0, 0, parts, SLOW_WINDOW)

    def share_pair(i):
        a, b = gather_pair(i)
        send_weight(x, a, gx_sem.at[0, i, 0], to_x_next)
        send_weight(x, b, gx_sem.at[1, i, 0], to_x_prev)
        send_weight(x, b, gx_sem.at[0, i, 1], to_x_next)
        send_weight(x, a, gx_sem.at[1, i, 1], to_x_prev)

    for i in range(half):
        share_pair(i)

    loads[2].wait()

    def norm_rows(g, carry):
        at = pl.ds(pl.multiple_of(g * ROW_GROUP, ROW_GROUP), ROW_GROUP)
        values, scale = normalize(xs[at, :].astype(jnp.float32))
        normed[at, :] = values
        hid[at, :] = values.astype(jnp.bfloat16)
        inverse[at, :] = jnp.broadcast_to(scale, (ROW_GROUP, 128))
        return carry

    lax.fori_loop(0, rows // ROW_GROUP, norm_rows, 0)
    for load in loads[3:]:
        load.wait()

    @pl.when(last)
    def _():
        def ready(i, carry):
            pl.semaphore_signal(top_ready, inc=1, device_id={"pipe": i}, device_id_type=MESH)
            return carry

        lax.fori_loop(0, n_pipe - 1, ready, 0)

    proj_sum[...] = jnp.zeros_like(proj_sum)
    head_sum[...] = jnp.zeros_like(head_sum)

    def use_blocks(places):
        project, output = 0.0, 0.0
        for xx, zz in places:
            s = xx * n_z + zz
            cols = pl.ds(pl.multiple_of(s * block, block), block)
            project += dot32(hid[:, cols], full[s, :, :pw])
            output += dot32(inc[:seq, cols], full[s, :, pw:])
        proj_sum[...] += project
        head_sum[...] += output

    def transpose_block(src, dst, b):
        dst[b * block : (b + 1) * block, :] = src[:, b * block : (b + 1) * block].T

    columns = (x, x_prev, x_next, x_far)
    steps = 2 * parts
    for i in range(steps + 3):
        if i < steps:
            a, b = gather_pair(i)
            if i >= half:
                weight_arrived(x, a)
                weight_arrived(x, b)
                z_items(parts + i - half, SLOW_WINDOW + i - half, 1, 1)
                share_pair(i)
        if 1 <= i <= steps:
            a, b = gather_pair(i - 1)
            weight_arrived(x_prev, a)
            send_weight(x_prev, a, gx_sem.at[0, i - 1, 2], to_x_next)
            weight_arrived(x_next, b)
            send_weight(x_next, b, gx_sem.at[1, i - 1, 2], to_x_prev)
        if i >= 3:
            a, b = gather_pair(i - 3)
            weight_arrived(x_prev, b)
            weight_arrived(x_next, a)
            weight_arrived(x_far, a)
            weight_arrived(x_far, b)
        if 1 <= i <= parts:
            for b in range(2 * i - 2, 2 * i):
                transpose_block(hid, hid_t, b)
        if i == half + 2:
            use_blocks([(xx, z) for xx in columns])
        if i == 3 * half + 2:
            use_blocks([(xx, zz) for xx in columns for zz in (z_prev, z_next)])
        if i == steps:
            use_blocks([(x, z_far)])

    my_cols = pl.ds(pl.multiple_of(p * (width // n_pipe), width // n_pipe), width // n_pipe)
    later = pl.ds(seq, seq)
    top_copy = pltpu.make_async_remote_copy(
        src_ref=topv,
        dst_ref=inc.at[later, my_cols],
        send_sem=top_send,
        recv_sem=top_recv.at[p],
        device_id={"pipe": n_pipe - 1},
        device_id_type=MESH,
    )

    @pl.when(jnp.logical_not(last))
    def _():
        pl.semaphore_wait(top_ready, 1)
        top_copy.start()

    use_blocks([(xx, z_far) for xx in (x_prev, x_next, x_far)])

    projected = proj_sum[...]
    query, query_scale = normalize(projected[:, :head])
    key, key_scale = normalize(projected[:, head : 2 * head])
    query_half = query.astype(jnp.bfloat16)
    key_half = key.astype(jnp.bfloat16)
    value_half = projected[:, 2 * head :].astype(jnp.bfloat16)
    attention = []
    for t in range(ticks):
        at = slice(t * seq, (t + 1) * seq)
        powered = jnp.exp(dot32(query_half[at], key_half[at], CONTRACT_LAST) / root)
        attention.append(powered / jnp.sum(powered, axis=-1, keepdims=True))
    attention_half = [a.astype(jnp.bfloat16) for a in attention]

    def head_back(t, head_grad):
        at = slice(t * seq, (t + 1) * seq)
        prob_grad = dot32(head_grad, value_half[at], CONTRACT_LAST)
        value_grad = dot32(attention_half[t], head_grad, CONTRACT_FIRST)
        weighted = attention[t]
        score_grad = (
            weighted
            * (prob_grad - jnp.sum(weighted * prob_grad, axis=-1, keepdims=True))
            / root
        ).astype(jnp.bfloat16)
        query_grad = dot32(score_grad, key_half[at])
        key_grad = dot32(score_grad, query_half[at], CONTRACT_FIRST)
        proj_grad[at, :head] = norm_back(query_grad, query[at], query_scale[at]).astype(
            jnp.bfloat16
        )
        proj_grad[at, head : 2 * head] = norm_back(key_grad, key[at], key_scale[at]).astype(
            jnp.bfloat16
        )
        proj_grad[at, 2 * head :] = value_grad.astype(jnp.bfloat16)

    def hidden_back(t, s):
        hg[:, s * block : (s + 1) * block] = dot32(
            proj_grad[t * seq : (t + 1) * seq, :], full[s, :, :pw], CONTRACT_LAST
        )

    def rows_back(t, g):
        at = slice(g * ROW_GROUP, (g + 1) * ROW_GROUP)
        both = slice(t * seq + g * ROW_GROUP, t * seq + (g + 1) * ROW_GROUP)
        grad = norm_back(hg[at, :], normed[both, :], inverse[both, :1])
        return (inc[both, :].astype(jnp.float32) + grad).astype(jnp.bfloat16)

    head_back(0, head_sum[...].astype(jnp.bfloat16))
    for s in range(n_x * n_z):
        hidden_back(0, s)
    groups = seq // ROW_GROUP
    back_copies = []
    for g in range(groups):
        at = pl.ds(g * ROW_GROUP, ROW_GROUP)
        sent_back[g * ROW_GROUP : (g + 1) * ROW_GROUP, :] = rows_back(0, g)
        back = pltpu.make_async_remote_copy(
            src_ref=sent_back.at[at],
            dst_ref=inc.at[pl.ds(seq + g * ROW_GROUP, ROW_GROUP)],
            send_sem=pass_send.at[g],
            recv_sem=pass_recv.at[g],
            device_id={"pipe": jnp.maximum(p - 1, 0)},
            device_id_type=MESH,
        )
        back_copies.append(back)

        @pl.when(p > 0)
        def _():
            back.start()

    for t in range(ticks):
        at = slice(t * seq, (t + 1) * seq)
        mixed[at, :] = dot32(attention_half[t], value_half[at]).astype(jnp.bfloat16)
    drain()
    for n in range(n_items):
        for way in range(2):
            sent(weight(x, z, 0), gz_sem.at[way, n])

    @pl.when(last)
    def _():
        top_width = width // n_pipe
        inc[seq:, (n_pipe - 1) * top_width :] = topv[...]

        def one(i, carry):
            cols = pl.ds(pl.multiple_of(i * top_width, top_width), top_width)
            arrived(inc.at[later, cols], top_recv.at[i])
            return carry

        lax.fori_loop(0, n_pipe - 1, one, 0)

    @pl.when(jnp.logical_not(last))
    def _():
        for g in range(groups):
            arrived(inc.at[pl.ds(seq + g * ROW_GROUP, ROW_GROUP)], pass_recv.at[g])

    head_grad = jnp.zeros((seq, head), jnp.float32)
    for s in range(n_x * n_z):
        head_grad += dot32(inc[seq:, s * block : (s + 1) * block], full[s, :, pw:])
        transpose_block(inc, inc_t, s)
    head_back(1, head_grad.astype(jnp.bfloat16))

    def scatter_pair(k):
        phase, j = divmod(k, half)
        za = (z_far, z_prev, z_next, z)[phase]
        zb = (z_far, z_next, z_prev, z)[phase]
        return ((za, j), (zb, half + j))

    around = (x, x_next, x_far, x_prev)
    OWN, NEXT, FAR, PREV = range(4)

    def make_parts(k):
        pieces = []
        for xx in around:
            for zz, c in scatter_pair(k):
                start = (xx * n_z + zz) * block + c * piece
                pieces.append(pl.ds(pl.multiple_of(start, piece), piece))
        projects = dot32(jnp.concatenate([hid_t[at, :] for at in pieces], axis=0), proj_grad[...])
        outputs = dot32(jnp.concatenate([inc_t[at, :] for at in pieces], axis=0), mixed[...])
        for n in range(len(pieces)):
            at = slice(n * piece, (n + 1) * piece)
            part[k, n // 2, n % 2, :, :pw] = projects[at].astype(jnp.bfloat16)
            part[k, n // 2, n % 2, :, pw:] = outputs[at].astype(jnp.bfloat16)

    def added(k, place, ab, relay):
        total = part[k, place, ab].astype(jnp.float32) + relay[...].astype(jnp.float32)
        part[k, place, ab] = total.astype(jnp.bfloat16)

    left, right, hidden_at = 0, 1, 0
    for i in range(steps + 3):
        if i < steps:
            make_parts(i)
            send(part.at[i, FAR, 0], x_relay.at[i, 0], sx_sem.at[i, 0], xr_sem.at[i, 0], to_x_next)
            send(part.at[i, FAR, 1], x_relay.at[i, 1], sx_sem.at[i, 1], xr_sem.at[i, 1], to_x_prev)
            send(
                part.at[i, NEXT, 1],
                x_final.at[i, left, 1],
                sx_sem.at[i, 2],
                xf_sem.at[i, left, 1],
                to_x_next,
            )
            send(
                part.at[i, PREV, 0],
                x_final.at[i, right, 0],
                sx_sem.at[i, 3],
                xf_sem.at[i, right, 0],
                to_x_prev,
            )
        if 1 <= i <= steps:
            k = i - 1
            arrived(x_relay.at[k, 0], xr_sem.at[k, 0])
            added(k, NEXT, 0, x_relay.at[k, 0])
            send(
                part.at[k, NEXT, 0],
                x_final.at[k, left, 0],
                sx_sem.at[k, 4],
                xf_sem.at[k, left, 0],
                to_x_next,
            )
            arrived(x_relay.at[k, 1], xr_sem.at[k, 1])
            added(k, PREV, 1, x_relay.at[k, 1])
            send(
                part.at[k, PREV, 1],
                x_final.at[k, right, 1],
                sx_sem.at[k, 5],
                xf_sem.at[k, right, 1],
                to_x_prev,
            )
        if i >= 3:
            k = i - 3
            phase, j = divmod(k, half)
            for ab in range(2):
                for way in (left, right):
                    arrived(x_final.at[k, way, ab], xf_sem.at[k, way, ab])
                total = (
                    part[k, OWN, ab].astype(jnp.float32)
                    + x_final[k, left, ab].astype(jnp.float32)
                    + x_final[k, right, ab].astype(jnp.float32)
                )
                if phase == 3:
                    own[half * ab + j] = total
                    continue
                if phase == 2:
                    arrived(z_relay.at[j, ab], zr_sem.at[j, ab])
                    total = total + z_relay[j, ab].astype(jnp.float32)
                z_send[k, ab] = total.astype(jnp.bfloat16)
                onward = ab == (1 if phase == 1 else 0)
                device = to_z_next if onward else to_z_prev
                if phase == 0:
                    send(
                        z_send.at[k, ab],
                        z_relay.at[j, ab],
                        sz_sem.at[k, ab],
                        zr_sem.at[j, ab],
                        device,
                    )
                else:
                    way, c = (left if onward else right, half * ab + j)
                    send(
                        z_send.at[k, ab],
                        z_final.at[way, c],
                        sz_sem.at[k, ab],
                        zf_sem.at[way, c],
                        device,
                    )
        if hidden_at < n_x * n_z:
            hidden_back(1, hidden_at)
            hidden_at += 1
    for s in range(hidden_at, n_x * n_z):
        hidden_back(1, s)
    for g in range(groups):
        pass_out[g * ROW_GROUP : (g + 1) * ROW_GROUP, :] = rows_back(1, g)
    for ab in (1, 0):
        for j in range(half):
            c = half * ab + j
            arrived(z_final.at[left, c], zf_sem.at[left, c])
            arrived(z_final.at[right, c], zf_sem.at[right, c])
            total = (
                own[c]
                + z_final[left, c].astype(jnp.float32)
                + z_final[right, c].astype(jnp.float32)
            )
            pg_out[c * piece : (c + 1) * piece, :] = total[:, :pw]
            og_out[c * piece : (c + 1) * piece, :] = total[:, pw:]
    drain()

    @pl.when(p > 0)
    def _():
        for back in back_copies:
            back.wait_send()

    @pl.when(jnp.logical_not(last))
    def _():
        top_copy.wait_send()


def put_out(pg_in, og_in, pass_in, pg_out, og_out, pass_out, sems):
    pairs = ((pg_in, pg_out), (og_in, og_out), (pass_in, pass_out))
    copies = [pltpu.make_async_copy(a, b, sems.at[n]) for n, (a, b) in enumerate(pairs)]
    for copy in copies:
        copy.start()
    for copy in copies:
        copy.wait()


def shards(n_pipe, n_x, n_z, section_inputs, arriving, top_grads, project_weights, output_weights):
    _, ticks, seq, width = section_inputs.shape
    head = output_weights.shape[2]
    rows = ticks * seq
    block = width // (n_x * n_z)
    piece = block // PARTS
    half, steps, wide = PARTS // 2, 2 * PARTS, 4 * head
    low, high = jnp.bfloat16, jnp.float32
    dma = pltpu.SemaphoreType.DMA
    scratch = [
        pltpu.VMEM((rows, width), low),
        pltpu.VMEM((rows, width), high),
        pltpu.VMEM((rows, 128), high),
        pltpu.VMEM((rows, width), low),
        pltpu.VMEM((width, rows), low),
        pltpu.VMEM((rows, width), low),
        pltpu.VMEM((width, rows), low),
        pltpu.VMEM((seq, width // n_pipe), low),
        pltpu.VMEM((n_x * n_z, block, wide), low),
        pltpu.VMEM((rows, 3 * head), high),
        pltpu.VMEM((seq, head), high),
        pltpu.VMEM((seq, width), high),
        pltpu.VMEM((seq, width), low),
        pltpu.VMEM((rows, 3 * head), low),
        pltpu.VMEM((rows, head), low),
        pltpu.VMEM((steps, 4, 2, piece, wide), low),
        pltpu.VMEM((steps, 2, piece, wide), low),
        pltpu.VMEM((steps, 2, 2, piece, wide), low),
        pltpu.VMEM((3 * half, 2, piece, wide), low),
        pltpu.VMEM((half, 2, piece, wide), low),
        pltpu.VMEM((2, PARTS, piece, wide), low),
        pltpu.VMEM((PARTS, piece, wide), high),
        dma((5,)),
        dma((n_x * n_z, PARTS)),
        dma((2, 3 * half)),
        dma((2, steps, 3)),
        dma((n_pipe,)),
        dma(()),
        dma((seq // ROW_GROUP,)),
        dma((seq // ROW_GROUP,)),
        dma((steps, 2)),
        dma((steps, 2, 2)),
        dma((half, 2)),
        dma((2, PARTS)),
        dma((steps, 6)),
        dma((3 * half, 2)),
        pltpu.SemaphoreType.REGULAR,
    ]
    anywhere = pl.BlockSpec(memory_space=pl.ANY)
    results = pl.pallas_call(
        functools.partial(kernel, (n_pipe, n_x, n_z, ticks, seq, width, head)),
        out_shape=(
            pltpu.VMEM((block, 3 * head), high),
            pltpu.VMEM((block, head), high),
            pltpu.VMEM((seq, width), low),
        ),
        in_specs=[pl.BlockSpec(memory_space=pltpu.HBM)] * 5,
        out_specs=[pl.BlockSpec(memory_space=pltpu.VMEM)] * 3,
        scratch_shapes=scratch,
        compiler_params=pltpu.CompilerParams(
            collective_id=0, has_side_effects=True, vmem_limit_bytes=65_900_000
        ),
    )(
        section_inputs.reshape(rows, width),
        arriving[0],
        top_grads[0],
        project_weights[0],
        output_weights[0],
    )
    project, output, passed = pl.pallas_call(
        put_out,
        out_shape=(
            jax.ShapeDtypeStruct((block, 3 * head), high),
            jax.ShapeDtypeStruct((block, head), high),
            jax.ShapeDtypeStruct((seq, width), low),
        ),
        in_specs=[pl.BlockSpec(memory_space=pltpu.VMEM)] * 3,
        out_specs=[anywhere] * 3,
        scratch_shapes=[dma((3,))],
        compiler_params=pltpu.CompilerParams(vmem_limit_bytes=4 * 1024 * 1024),
    )(*results)
    return (project[None], output[None], passed[None])


def solution(mesh):
    n_x = n_z = 4
    split = Mesh(mesh.devices.reshape(mesh.shape["pipe"], n_x, n_z), ("pipe", "dp_0", "dp_1"))
    in_specs = (
        P("pipe", None, DP, None),
        P("pipe", DP, None),
        P(None, DP, "pipe"),
        P("pipe", DP, None),
        P("pipe", DP, None),
    )
    out_specs = (P("pipe", DP, None), P("pipe", DP, None), P("pipe", DP, None))
    return jax.shard_map(
        functools.partial(shards, mesh.shape["pipe"], n_x, n_z),
        mesh=split,
        in_specs=in_specs,
        out_specs=out_specs,
        check_vma=False,
    )
```

```python
import functools
import math

import jax
import jax.numpy as jnp
from jax import lax
from jax.experimental import pallas as pl
from jax.experimental.pallas import tpu as pltpu
from jax.sharding import Mesh
from jax.sharding import PartitionSpec as P

DP = ("dp_0", "dp_1")
MESH = pl.DeviceIdType.MESH
EPSILON = 1e-06
PARTS = 8
WINDOWS = ((8, 2), (4, 3), (4, 3), (4, 2))
ROW_GROUP = 16
CONTRACT_FIRST = (((0,), (0,)), ((), ()))
CONTRACT_LAST = (((1,), (1,)), ((), ()))


def normalize(values):
    centered = values - jnp.mean(values, axis=-1, keepdims=True)
    inverse = lax.rsqrt(jnp.mean(centered * centered, axis=-1, keepdims=True) + EPSILON)
    return (centered * inverse, inverse)


def norm_back(gradient, normed, inverse):
    centered = gradient - jnp.mean(gradient, axis=-1, keepdims=True)
    return inverse * (centered - normed * jnp.mean(gradient * normed, axis=-1, keepdims=True))


def dot32(a, b, dims=None):
    if dims is None:
        return jnp.dot(a, b, preferred_element_type=jnp.float32)
    return lax.dot_general(a, b, dims, preferred_element_type=jnp.float32)


def kernel(
    dims,
    xin,
    arr,
    top,
    wp,
    wo,
    pg_out,
    og_out,
    pass_out,
    xs,
    normed,
    inverse,
    hid,
    hid_t,
    inc,
    inc_t,
    topv,
    full,
    proj_sum,
    head_sum,
    hg,
    sent_back,
    proj_grad,
    mixed,
    part,
    x_relay,
    x_final,
    z_send,
    z_relay,
    z_final,
    own,
    load_sem,
    gather_sem,
    gz_sem,
    gx_sem,
    top_recv,
    top_send,
    pass_recv,
    pass_send,
    xr_sem,
    xf_sem,
    zr_sem,
    zf_sem,
    sx_sem,
    sz_sem,
    top_ready,
):
    n_pipe, n_x, n_z, ticks, seq, width, head = dims
    parts, half = PARTS, PARTS // 2
    rows = ticks * seq
    block = width // (n_x * n_z)
    piece = block // parts
    wide = 4 * head
    pw = 3 * head
    root = math.sqrt(head)
    p = lax.axis_index("pipe")
    x = lax.axis_index("dp_0")
    z = lax.axis_index("dp_1")
    x_next, x_prev, x_far = (lax.rem(x + s, n_x) for s in (1, n_x - 1, 2))
    z_next, z_prev, z_far = (lax.rem(z + s, n_z) for s in (1, n_z - 1, 2))
    last = p == n_pipe - 1
    to_x_next, to_x_prev = ({"dp_0": x_next}, {"dp_0": x_prev})
    to_z_next, to_z_prev = ({"dp_1": z_next}, {"dp_1": z_prev})
    pending = []

    def send(src, dst, send_sem, recv_sem, device, keep=True):
        copy = pltpu.make_async_remote_copy(
            src_ref=src,
            dst_ref=dst,
            send_sem=send_sem,
            recv_sem=recv_sem,
            device_id=device,
            device_id_type=MESH,
        )
        copy.start()
        if keep:
            pending.append(copy)

    def arrived(dst, recv_sem):
        pltpu.make_async_remote_copy(
            src_ref=dst,
            dst_ref=dst,
            send_sem=recv_sem,
            recv_sem=recv_sem,
            device_id=to_x_next,
            device_id_type=MESH,
        ).wait_recv()

    def sent(src, send_sem):
        pltpu.make_async_remote_copy(
            src_ref=src,
            dst_ref=src,
            send_sem=send_sem,
            recv_sem=send_sem,
            device_id=to_x_next,
            device_id_type=MESH,
        ).wait_send()

    def drain():
        for copy in pending:
            copy.wait_send()
        pending.clear()

    me = x * n_z + z
    loads = [
        pltpu.make_async_copy(wp, full.at[me, :, pl.ds(0, pw)], load_sem.at[0]),
        pltpu.make_async_copy(wo, full.at[me, :, pl.ds(pw, head)], load_sem.at[1]),
        pltpu.make_async_copy(xin, xs, load_sem.at[2]),
        pltpu.make_async_copy(arr, inc.at[pl.ds(0, seq)], load_sem.at[3]),
        pltpu.make_async_copy(top, topv, load_sem.at[4]),
    ]
    for load in loads:
        load.start()

    barrier = pltpu.get_barrier_semaphore()
    for device in (to_x_next, to_x_prev, to_z_next, to_z_prev):
        pl.semaphore_signal(barrier, inc=1, device_id=device, device_id_type=MESH)

    @pl.when(p > 0)
    def _():
        pl.semaphore_signal(barrier, inc=1, device_id={"pipe": p - 1}, device_id_type=MESH)

    @pl.when(p < n_pipe - 1)
    def _():
        pl.semaphore_signal(barrier, inc=1, device_id={"pipe": p + 1}, device_id_type=MESH)
        pl.semaphore_signal(barrier, inc=1, device_id={"pipe": n_pipe - 1}, device_id_type=MESH)

    loads[0].wait()
    loads[1].wait()
    from_neighbours = 4 + jnp.where(p > 0, 1, 0) + jnp.where(last, n_pipe - 1, 1)
    pl.semaphore_wait(barrier, from_neighbours)

    def weight(xx, zz, c):
        return full.at[xx * n_z + zz, pl.ds(c * piece, piece), :]

    def weight_sem(xx, zz, c):
        return gather_sem.at[xx * n_z + zz, c]

    def gather_pair(k):
        phase, j = divmod(k, half)
        za = (z, z_prev, z_next, z_far)[phase]
        zb = (z, z_next, z_prev, z_far)[phase]
        return ((za, j), (zb, half + j))

    def send_weight(xx, at, sem, device, keep=True):
        zz, c = at
        send(weight(xx, zz, c), weight(xx, zz, c), sem, weight_sem(xx, zz, c), device, keep)

    def weight_arrived(xx, at):
        zz, c = at
        arrived(weight(xx, zz, c), weight_sem(xx, zz, c))

    place = lax.rem(p // 2, len(WINDOWS))
    window_of = {}
    for spot, windows in enumerate(WINDOWS):
        for core, window in enumerate(windows):
            here = jnp.logical_and(place == spot, lax.rem(p, 2) == core)
            known = window_of.get(window)
            window_of[window] = here if known is None else jnp.logical_or(known, here)
    n_items = parts + half

    def z_item(n):
        if n < half:
            up, down = (z, n), (z, half + n)
        elif n < parts:
            up, down = (z, n), (z, n - half)
        else:
            up, down = gather_pair(half + n - parts)
        send_weight(x, up, gz_sem.at[0, n], to_z_next, False)
        send_weight(x, down, gz_sem.at[1, n], to_z_prev, False)

    def z_items(first, stop):
        for window, here in window_of.items():

            @pl.when(here)
            def _():
                for n in range(max(window + first, 0), min(window + stop, n_items)):
                    z_item(n)

    z_items(-n_items, 0)

    def share_pair(i):
        a, b = gather_pair(i)
        send_weight(x, a, gx_sem.at[0, i, 0], to_x_next)
        send_weight(x, b, gx_sem.at[1, i, 0], to_x_prev)
        send_weight(x, b, gx_sem.at[0, i, 1], to_x_next)
        send_weight(x, a, gx_sem.at[1, i, 1], to_x_prev)

    for i in range(half):
        share_pair(i)

    loads[2].wait()

    def norm_rows(g, carry):
        at = pl.ds(pl.multiple_of(g * ROW_GROUP, ROW_GROUP), ROW_GROUP)
        values, scale = normalize(xs[at, :].astype(jnp.float32))
        normed[at, :] = values
        hid[at, :] = values.astype(jnp.bfloat16)
        inverse[at, :] = jnp.broadcast_to(scale, (ROW_GROUP, 128))
        return carry

    lax.fori_loop(0, rows // ROW_GROUP, norm_rows, 0)
    for load in loads[3:]:
        load.wait()

    @pl.when(last)
    def _():
        def ready(i, carry):
            pl.semaphore_signal(top_ready, inc=1, device_id={"pipe": i}, device_id_type=MESH)
            return carry

        lax.fori_loop(0, n_pipe - 1, ready, 0)

    proj_sum[...] = jnp.zeros_like(proj_sum)
    head_sum[...] = jnp.zeros_like(head_sum)

    def use_blocks(places):
        project, output = 0.0, 0.0
        for xx, zz in places:
            s = xx * n_z + zz
            cols = pl.ds(pl.multiple_of(s * block, block), block)
            project += dot32(hid[:, cols], full[s, :, :pw])
            output += dot32(inc[:seq, cols], full[s, :, pw:])
        proj_sum[...] += project
        head_sum[...] += output

    def transpose_block(src, dst, b):
        dst[b * block : (b + 1) * block, :] = src[:, b * block : (b + 1) * block].T

    columns = (x, x_prev, x_next, x_far)
    steps = 2 * parts
    for i in range(steps + 3):
        if i < steps:
            a, b = gather_pair(i)
            if i >= half:
                weight_arrived(x, a)
                weight_arrived(x, b)
                z_items(i - half, i - half + 1)
                share_pair(i)
        if 1 <= i <= steps:
            a, b = gather_pair(i - 1)
            weight_arrived(x_prev, a)
            send_weight(x_prev, a, gx_sem.at[0, i - 1, 2], to_x_next)
            weight_arrived(x_next, b)
            send_weight(x_next, b, gx_sem.at[1, i - 1, 2], to_x_prev)
        if i >= 3:
            a, b = gather_pair(i - 3)
            weight_arrived(x_prev, b)
            weight_arrived(x_next, a)
            weight_arrived(x_far, a)
            weight_arrived(x_far, b)
        if 1 <= i <= parts:
            for b in range(2 * i - 2, 2 * i):
                transpose_block(hid, hid_t, b)
        if i == half + 2:
            use_blocks([(xx, z) for xx in columns])
        if i == 3 * half + 2:
            use_blocks([(xx, zz) for xx in columns for zz in (z_prev, z_next)])
        if i == steps:
            use_blocks([(x, z_far)])

    my_cols = pl.ds(pl.multiple_of(p * (width // n_pipe), width // n_pipe), width // n_pipe)
    later = pl.ds(seq, seq)
    top_copy = pltpu.make_async_remote_copy(
        src_ref=topv,
        dst_ref=inc.at[later, my_cols],
        send_sem=top_send,
        recv_sem=top_recv.at[p],
        device_id={"pipe": n_pipe - 1},
        device_id_type=MESH,
    )

    @pl.when(jnp.logical_not(last))
    def _():
        pl.semaphore_wait(top_ready, 1)
        top_copy.start()

    use_blocks([(xx, z_far) for xx in (x_prev, x_next, x_far)])

    projected = proj_sum[...]
    query, query_scale = normalize(projected[:, :head])
    key, key_scale = normalize(projected[:, head : 2 * head])
    query_half = query.astype(jnp.bfloat16)
    key_half = key.astype(jnp.bfloat16)
    value_half = projected[:, 2 * head :].astype(jnp.bfloat16)
    attention = []
    for t in range(ticks):
        at = slice(t * seq, (t + 1) * seq)
        powered = jnp.exp(dot32(query_half[at], key_half[at], CONTRACT_LAST) / root)
        attention.append(powered / jnp.sum(powered, axis=-1, keepdims=True))
    attention_half = [a.astype(jnp.bfloat16) for a in attention]

    def head_back(t, head_grad):
        at = slice(t * seq, (t + 1) * seq)
        prob_grad = dot32(head_grad, value_half[at], CONTRACT_LAST)
        value_grad = dot32(attention_half[t], head_grad, CONTRACT_FIRST)
        weighted = attention[t]
        score_grad = (
            weighted
            * (prob_grad - jnp.sum(weighted * prob_grad, axis=-1, keepdims=True))
            / root
        ).astype(jnp.bfloat16)
        query_grad = dot32(score_grad, key_half[at])
        key_grad = dot32(score_grad, query_half[at], CONTRACT_FIRST)
        proj_grad[at, :head] = norm_back(query_grad, query[at], query_scale[at]).astype(
            jnp.bfloat16
        )
        proj_grad[at, head : 2 * head] = norm_back(key_grad, key[at], key_scale[at]).astype(
            jnp.bfloat16
        )
        proj_grad[at, 2 * head :] = value_grad.astype(jnp.bfloat16)

    def hidden_back(t, s):
        hg[:, s * block : (s + 1) * block] = dot32(
            proj_grad[t * seq : (t + 1) * seq, :], full[s, :, :pw], CONTRACT_LAST
        )

    def rows_back(t, g):
        at = slice(g * ROW_GROUP, (g + 1) * ROW_GROUP)
        both = slice(t * seq + g * ROW_GROUP, t * seq + (g + 1) * ROW_GROUP)
        grad = norm_back(hg[at, :], normed[both, :], inverse[both, :1])
        return (inc[both, :].astype(jnp.float32) + grad).astype(jnp.bfloat16)

    head_back(0, head_sum[...].astype(jnp.bfloat16))
    for s in range(n_x * n_z):
        hidden_back(0, s)
    groups = seq // ROW_GROUP
    back_copies = []
    for g in range(groups):
        at = pl.ds(g * ROW_GROUP, ROW_GROUP)
        sent_back[g * ROW_GROUP : (g + 1) * ROW_GROUP, :] = rows_back(0, g)
        back = pltpu.make_async_remote_copy(
            src_ref=sent_back.at[at],
            dst_ref=inc.at[pl.ds(seq + g * ROW_GROUP, ROW_GROUP)],
            send_sem=pass_send.at[g],
            recv_sem=pass_recv.at[g],
            device_id={"pipe": jnp.maximum(p - 1, 0)},
            device_id_type=MESH,
        )
        back_copies.append(back)

        @pl.when(p > 0)
        def _():
            back.start()

    for t in range(ticks):
        at = slice(t * seq, (t + 1) * seq)
        mixed[at, :] = dot32(attention_half[t], value_half[at]).astype(jnp.bfloat16)
    drain()
    for n in range(n_items):
        for way in range(2):
            sent(weight(x, z, 0), gz_sem.at[way, n])

    @pl.when(last)
    def _():
        top_width = width // n_pipe
        inc[seq:, (n_pipe - 1) * top_width :] = topv[...]

        def one(i, carry):
            cols = pl.ds(pl.multiple_of(i * top_width, top_width), top_width)
            arrived(inc.at[later, cols], top_recv.at[i])
            return carry

        lax.fori_loop(0, n_pipe - 1, one, 0)

    @pl.when(jnp.logical_not(last))
    def _():
        for g in range(groups):
            arrived(inc.at[pl.ds(seq + g * ROW_GROUP, ROW_GROUP)], pass_recv.at[g])

    head_grad = jnp.zeros((seq, head), jnp.float32)
    for s in range(n_x * n_z):
        head_grad += dot32(inc[seq:, s * block : (s + 1) * block], full[s, :, pw:])
        transpose_block(inc, inc_t, s)
    head_back(1, head_grad.astype(jnp.bfloat16))

    def scatter_pair(k):
        phase, j = divmod(k, half)
        za = (z_far, z_prev, z_next, z)[phase]
        zb = (z_far, z_next, z_prev, z)[phase]
        return ((za, j), (zb, half + j))

    around = (x, x_next, x_far, x_prev)
    OWN, NEXT, FAR, PREV = range(4)

    def make_parts(k):
        pieces = []
        for xx in around:
            for zz, c in scatter_pair(k):
                start = (xx * n_z + zz) * block + c * piece
                pieces.append(pl.ds(pl.multiple_of(start, piece), piece))
        projects = dot32(jnp.concatenate([hid_t[at, :] for at in pieces], axis=0), proj_grad[...])
        outputs = dot32(jnp.concatenate([inc_t[at, :] for at in pieces], axis=0), mixed[...])
        for n in range(len(pieces)):
            at = slice(n * piece, (n + 1) * piece)
            part[k, n // 2, n % 2, :, :pw] = projects[at].astype(jnp.bfloat16)
            part[k, n // 2, n % 2, :, pw:] = outputs[at].astype(jnp.bfloat16)

    def added(k, place, ab, relay):
        total = part[k, place, ab].astype(jnp.float32) + relay[...].astype(jnp.float32)
        part[k, place, ab] = total.astype(jnp.bfloat16)

    left, right, hidden_at = 0, 1, 0

    def finish(k):
        phase, j = divmod(k, half)
        for ab in range(2):
            for way in (left, right):
                arrived(x_final.at[k, way, ab], xf_sem.at[k, way, ab])
            total = (
                part[k, OWN, ab].astype(jnp.float32)
                + x_final[k, left, ab].astype(jnp.float32)
                + x_final[k, right, ab].astype(jnp.float32)
            )
            if phase == 3:
                own[half * ab + j] = total
                continue
            if phase == 2:
                arrived(z_relay.at[j, ab], zr_sem.at[j, ab])
                total = total + z_relay[j, ab].astype(jnp.float32)
            z_send[k, ab] = total.astype(jnp.bfloat16)
            onward = ab == (1 if phase == 1 else 0)
            device = to_z_next if onward else to_z_prev
            if phase == 0:
                send(
                    z_send.at[k, ab],
                    z_relay.at[j, ab],
                    sz_sem.at[k, ab],
                    zr_sem.at[j, ab],
                    device,
                )
            else:
                way, c = (left if onward else right, half * ab + j)
                send(
                    z_send.at[k, ab],
                    z_final.at[way, c],
                    sz_sem.at[k, ab],
                    zf_sem.at[way, c],
                    device,
                )

    for i in range(steps + 3):
        if i < steps:
            make_parts(i)
            send(part.at[i, FAR, 0], x_relay.at[i, 0], sx_sem.at[i, 0], xr_sem.at[i, 0], to_x_next)
            send(part.at[i, FAR, 1], x_relay.at[i, 1], sx_sem.at[i, 1], xr_sem.at[i, 1], to_x_prev)
            send(
                part.at[i, NEXT, 1],
                x_final.at[i, left, 1],
                sx_sem.at[i, 2],
                xf_sem.at[i, left, 1],
                to_x_next,
            )
            send(
                part.at[i, PREV, 0],
                x_final.at[i, right, 0],
                sx_sem.at[i, 3],
                xf_sem.at[i, right, 0],
                to_x_prev,
            )
        if 1 <= i <= steps:
            k = i - 1
            arrived(x_relay.at[k, 0], xr_sem.at[k, 0])
            added(k, NEXT, 0, x_relay.at[k, 0])
            send(
                part.at[k, NEXT, 0],
                x_final.at[k, left, 0],
                sx_sem.at[k, 4],
                xf_sem.at[k, left, 0],
                to_x_next,
            )
            arrived(x_relay.at[k, 1], xr_sem.at[k, 1])
            added(k, PREV, 1, x_relay.at[k, 1])
            send(
                part.at[k, PREV, 1],
                x_final.at[k, right, 1],
                sx_sem.at[k, 5],
                xf_sem.at[k, right, 1],
                to_x_prev,
            )
        if i >= 3:
            finish(i - 3)
        if hidden_at < n_x * n_z:
            hidden_back(1, hidden_at)
            hidden_at += 1
    for s in range(hidden_at, n_x * n_z):
        hidden_back(1, s)
    for g in range(groups):
        pass_out[g * ROW_GROUP : (g + 1) * ROW_GROUP, :] = rows_back(1, g)
    for ab in (1, 0):
        for j in range(half):
            c = half * ab + j
            arrived(z_final.at[left, c], zf_sem.at[left, c])
            arrived(z_final.at[right, c], zf_sem.at[right, c])
            total = (
                own[c]
                + z_final[left, c].astype(jnp.float32)
                + z_final[right, c].astype(jnp.float32)
            )
            pg_out[c * piece : (c + 1) * piece, :] = total[:, :pw]
            og_out[c * piece : (c + 1) * piece, :] = total[:, pw:]
    drain()

    @pl.when(p > 0)
    def _():
        for back in back_copies:
            back.wait_send()

    @pl.when(jnp.logical_not(last))
    def _():
        top_copy.wait_send()


def put_out(pg_in, og_in, pass_in, pg_out, og_out, pass_out, sems):
    pairs = ((pg_in, pg_out), (og_in, og_out), (pass_in, pass_out))
    copies = [pltpu.make_async_copy(a, b, sems.at[n]) for n, (a, b) in enumerate(pairs)]
    for copy in copies:
        copy.start()
    for copy in copies:
        copy.wait()


def shards(n_pipe, n_x, n_z, section_inputs, arriving, top_grads, project_weights, output_weights):
    _, ticks, seq, width = section_inputs.shape
    head = output_weights.shape[2]
    rows = ticks * seq
    block = width // (n_x * n_z)
    piece = block // PARTS
    half, steps, wide = PARTS // 2, 2 * PARTS, 4 * head
    low, high = jnp.bfloat16, jnp.float32
    dma = pltpu.SemaphoreType.DMA
    scratch = [
        pltpu.VMEM((rows, width), low),
        pltpu.VMEM((rows, width), high),
        pltpu.VMEM((rows, 128), high),
        pltpu.VMEM((rows, width), low),
        pltpu.VMEM((width, rows), low),
        pltpu.VMEM((rows, width), low),
        pltpu.VMEM((width, rows), low),
        pltpu.VMEM((seq, width // n_pipe), low),
        pltpu.VMEM((n_x * n_z, block, wide), low),
        pltpu.VMEM((rows, 3 * head), high),
        pltpu.VMEM((seq, head), high),
        pltpu.VMEM((seq, width), high),
        pltpu.VMEM((seq, width), low),
        pltpu.VMEM((rows, 3 * head), low),
        pltpu.VMEM((rows, head), low),
        pltpu.VMEM((steps, 4, 2, piece, wide), low),
        pltpu.VMEM((steps, 2, piece, wide), low),
        pltpu.VMEM((steps, 2, 2, piece, wide), low),
        pltpu.VMEM((3 * half, 2, piece, wide), low),
        pltpu.VMEM((half, 2, piece, wide), low),
        pltpu.VMEM((2, PARTS, piece, wide), low),
        pltpu.VMEM((PARTS, piece, wide), high),
        dma((5,)),
        dma((n_x * n_z, PARTS)),
        dma((2, 3 * half)),
        dma((2, steps, 3)),
        dma((n_pipe,)),
        dma(()),
        dma((seq // ROW_GROUP,)),
        dma((seq // ROW_GROUP,)),
        dma((steps, 2)),
        dma((steps, 2, 2)),
        dma((half, 2)),
        dma((2, PARTS)),
        dma((steps, 6)),
        dma((3 * half, 2)),
        pltpu.SemaphoreType.REGULAR,
    ]
    anywhere = pl.BlockSpec(memory_space=pl.ANY)
    results = pl.pallas_call(
        functools.partial(kernel, (n_pipe, n_x, n_z, ticks, seq, width, head)),
        out_shape=(
            pltpu.VMEM((block, 3 * head), high),
            pltpu.VMEM((block, head), high),
            pltpu.VMEM((seq, width), low),
        ),
        in_specs=[pl.BlockSpec(memory_space=pltpu.HBM)] * 5,
        out_specs=[pl.BlockSpec(memory_space=pltpu.VMEM)] * 3,
        scratch_shapes=scratch,
        compiler_params=pltpu.CompilerParams(
            collective_id=0, has_side_effects=True, vmem_limit_bytes=65_900_000
        ),
    )(
        section_inputs.reshape(rows, width),
        arriving[0],
        top_grads[0],
        project_weights[0],
        output_weights[0],
    )
    project, output, passed = pl.pallas_call(
        put_out,
        out_shape=(
            jax.ShapeDtypeStruct((block, 3 * head), high),
            jax.ShapeDtypeStruct((block, head), high),
            jax.ShapeDtypeStruct((seq, width), low),
        ),
        in_specs=[pl.BlockSpec(memory_space=pltpu.VMEM)] * 3,
        out_specs=[anywhere] * 3,
        scratch_shapes=[dma((3,))],
        compiler_params=pltpu.CompilerParams(vmem_limit_bytes=4 * 1024 * 1024),
    )(*results)
    return (project[None], output[None], passed[None])


def solution(mesh):
    n_x = n_z = 4
    split = Mesh(mesh.devices.reshape(mesh.shape["pipe"], n_x, n_z), ("pipe", "dp_0", "dp_1"))
    in_specs = (
        P("pipe", None, DP, None),
        P("pipe", DP, None),
        P(None, DP, "pipe"),
        P("pipe", DP, None),
        P("pipe", DP, None),
    )
    out_specs = (P("pipe", DP, None), P("pipe", DP, None), P("pipe", DP, None))
    return jax.shard_map(
        functools.partial(shards, mesh.shape["pipe"], n_x, n_z),
        mesh=split,
        in_specs=in_specs,
        out_specs=out_specs,
        check_vma=False,
    )
```
